32 devices in a mesh: dp: 16 (over z, y, x), band: 2 (over core).
Axes of the slice: x: 2, y: 2, z: 4, core: 2. Of those that a mesh axis runs over, the one named last changes fastest.
Arguments:
- spectra: bfloat16 [224, 1024, 256], P('band', 'dp'), may hold values from -6 to 6
- first_spectral_weight: bfloat16 [3, 256, 256], replicated, may hold values from -0.21875 to 0.21875
- second_spectral_weight: bfloat16 [3, 256, 256], replicated, may hold values from -0.21875 to 0.21875
- patch_w: float32 [4, 256], replicated, may hold values from -3 to 3
- cotangent: bfloat16 [224, 256, 256], P('band', 'dp'), may hold values from -6 to 6
Outputs:
- spectra_gradient: bfloat16 [224, 1024, 256], P('band', 'dp')
- grad_first: float32 [256, 3, 256], P('dp')
- grad_second: float32 [256, 3, 256], P('dp')
- grad_patch: float32 [4, 256], replicated
The draws below stay inside these ranges and needn't reach their ends.
All inputs are finite; a program needn't handle non-finite values.
Results may differ from the reference program's by a relative error of at most 0.014.
Values may be sent and summed in bfloat16 or wider, within the bound.
A program may use at most 128 MiB of HBM per device.

```python
import math
import jax
import jax.numpy as jnp
from jax import lax

C = 256
BANDS = 224
BAND_DILATION_1 = 1
BAND_DILATION_2 = 2
PIXELS = 1024


def spiked(array, rng, source, target, shards_of, factor):
    owner, partner = [(jnp.arange(array.shape[position]) // (array.shape[position] // shards_of)).reshape([-1 if axis == position else 1 for axis in range(array.ndim)]) for position in (source, target)]
    chosen = jax.random.permutation(rng, shards_of)[partner]
    strong = (owner == chosen) | (owner == (partner + shards_of // 2) % shards_of)
    return jnp.where(strong, factor * array, array)


def steps_of(rng, extent, pieces, low, high):
    def one(axis_at, parts):
        steps = jax.random.uniform(jax.random.fold_in(jax.random.fold_in(rng, 6), axis_at), (parts,), jnp.float32, low / len(pieces), high / len(pieces))
        return jnp.repeat(jnp.exp(steps), extent[axis_at] // parts).reshape((-1,) + (1,) * (len(extent) - axis_at - 1))

    gain = one(*pieces[0])
    for cut in pieces[1:]:
        gain = gain * one(*cut)
    return gain


def bell_draw(rng, dims, spread, most, shards=(), kind=jnp.bfloat16):
    entries = spread * jax.random.normal(rng, dims, jnp.float32)
    if shards:
        entries = entries * steps_of(rng, dims, shards, -0.22, 0.18)
    return jnp.clip(entries, -most, most).astype(kind)


def gaussian_with(own_key, extent, scale, limit, cuts, heavy, kind=jnp.bfloat16):
    drawn = scale * jax.random.normal(own_key, extent, jnp.float32)
    if cuts:
        drawn = drawn * steps_of(own_key, extent, cuts, -0.22, 0.18)
    return jnp.clip(spiked(drawn, jax.random.fold_in(own_key, 3), *heavy), -limit, limit).astype(kind)


def setup_inputs(seed: int = 0) -> dict:
    keys = jax.random.split(jax.random.key(seed), 6)
    spectra = bell_draw(keys[0], (BANDS, PIXELS, C), 1.0, 6.0, ((0, 2), (1, 16)))
    first_spectral_weight = bell_draw(keys[1], (3, C, C), (3 * C) ** -0.5, 0.21875)
    second_spectral_weight = bell_draw(keys[2], (3, C, C), (3 * C) ** -0.5, 0.21875)
    patch_w = bell_draw(keys[3], (4, C), 4 ** -0.5, 3.0, (), jnp.float32)
    cotangent = gaussian_with(keys[4], (BANDS, PIXELS // 4, C), 1.0, 6.0, ((0, 2), (1, 16)), (1, 2, 16, 2.0))
    return dict(spectra=spectra, first_spectral_weight=first_spectral_weight, second_spectral_weight=second_spectral_weight, patch_w=patch_w, cotangent=cotangent)


def gelu_pair(field):
    value, pull = jax.vjp(jax.nn.gelu, field)
    return (value, pull(jnp.ones_like(field))[0])

def gather_tap_windows(field, dilation, flipped):
    tap_count = field.shape[0]
    padded = jnp.pad(field, ((dilation, dilation), (0, 0), (0, 0)))
    if flipped:
        starts = [dilation * (2 - tap_index) for tap_index in range(3)]
    else:
        starts = [dilation * tap_index for tap_index in range(3)]
    return jnp.concatenate([padded[s:s + tap_count] for s in starts], axis=-1)

def channel_mixing(taps, kernel):
    width = kernel.shape[1]
    out = jnp.dot(taps.reshape(-1, 3 * width), kernel.reshape(3 * width, kernel.shape[2]), preferred_element_type=jnp.float32)
    return out.reshape(taps.shape[0], taps.shape[1], -1)

def kernel_grad(delta, taps):
    width = delta.shape[2]
    out = lax.dot_general(delta.reshape(-1, width), taps.reshape(-1, 3 * width), (((0,), (0,)), ((), ())), preferred_element_type=jnp.float32)
    return out.reshape(width, 3, width)

def layer_pair(input_spectra, cotangent, first_spectral_weight, second_spectral_weight, patch_w):
    bands, pixels, width = input_spectra.shape
    first_tap_windows = gather_tap_windows(input_spectra, BAND_DILATION_1, False)
    h_one = channel_mixing(first_tap_windows, first_spectral_weight)
    u_one, slope_one = gelu_pair(h_one)
    first_preactivation = lax.optimization_barrier(jnp.sum(u_one.reshape(bands, pixels // 4, 4, width) * patch_w, axis=2)).astype(jnp.bfloat16)
    second_tap_windows = gather_tap_windows(first_preactivation, BAND_DILATION_2, False)
    h_two = channel_mixing(second_tap_windows, second_spectral_weight)
    unused, slope_two = gelu_pair(h_two)
    second_delta = (cotangent.astype(jnp.float32) * slope_two).astype(jnp.bfloat16)
    grad_two = kernel_grad(second_delta, second_tap_windows)
    backward_second_layer = channel_mixing(gather_tap_windows(second_delta, BAND_DILATION_2, True), jnp.transpose(second_spectral_weight, (0, 2, 1)))
    expanded = backward_second_layer[:, :, None, :]
    grad_patch = lax.optimization_barrier(jnp.sum(expanded * u_one.reshape(bands, pixels // 4, 4, width), axis=(0, 1)))
    first_delta = ((expanded * patch_w).reshape(bands, pixels, width) * slope_one).astype(jnp.bfloat16)
    grad_one = kernel_grad(first_delta, first_tap_windows)
    backward_first_layer = channel_mixing(gather_tap_windows(first_delta, BAND_DILATION_1, True), jnp.transpose(first_spectral_weight, (0, 2, 1))).astype(jnp.bfloat16)
    return (backward_first_layer, grad_one, grad_two, grad_patch)

def reference(spectra, first_spectral_weight, second_spectral_weight, patch_w, cotangent):
    bands, total, width = spectra.shape
    block = math.gcd(total, 512)
    tap_count = total // block

    def advance(carry, index):
        start = index * block
        piece = lax.dynamic_slice_in_dim(spectra, start, block, 1)
        cot_piece = lax.dynamic_slice_in_dim(cotangent, start // 4, block // 4, 1)
        back, grad_one, grad_two, grad_patch = layer_pair(piece, cot_piece, first_spectral_weight, second_spectral_weight, patch_w)
        return ((carry[0] + grad_one, carry[1] + grad_two, carry[2] + grad_patch), back)
    zero_kernel = jnp.zeros((width, 3, width), jnp.float32)
    init = (zero_kernel, zero_kernel, jnp.zeros((4, width), jnp.float32))
    sums, blocks = lax.scan(advance, init, jnp.arange(tap_count, dtype=jnp.int32))
    spectra_gradient = jnp.transpose(blocks, (1, 0, 2, 3)).reshape(bands, total, width)
    scale = 1.0 / math.sqrt(bands * total)
    return (spectra_gradient, sums[0] * scale, sums[1] * scale, sums[2] * scale)
```

```python
import functools
import math

import jax
import jax.numpy as jnp
from jax import lax
from jax.experimental import pallas as pl
from jax.experimental.pallas import tpu as pltpu
from jax.sharding import PartitionSpec as P

D1 = 1
D2 = 2
HZ = 1 + 2 * D2
HX = HZ + D1
HC = 1 + D2
MESH = pl.DeviceIdType.MESH
F32 = jnp.float32
BF16 = jnp.bfloat16
G0 = math.sqrt(2.0 / math.pi)
G1 = 0.044715 * G0


def divisor(n, most):
    return max(i for i in range(1, min(n, most) + 1) if n % i == 0)


def gelu_terms(v):
    sq = v * v
    p = 0.5 + 0.5 * jnp.tanh(v * (G0 + G1 * sq))
    u = v * p
    s = p + u * (1.0 - p) * (2.0 * G0 + (6.0 * G1) * sq)
    return u, s


def dot(a, b):
    return jnp.dot(a, b, preferred_element_type=F32)


def dot_rows(a, b):
    return lax.dot_general(a, b, (((0,), (0,)), ((), ())), preferred_element_type=F32)


def stacked(ref, starts, n):
    c = ref.shape[-1]
    return jnp.concatenate([ref[pl.ds(s, n)].reshape(-1, c) for s in starts], axis=-1)


def copy_in(pairs, sems):
    copies = [pltpu.make_async_copy(a, b, sems.at[i]) for i, (a, b) in enumerate(pairs)]
    for c in copies:
        c.start()
    return copies


def turn_weights(w1_ref, w2_ref, w1t, w2t):
    C = w1_ref.shape[-1]
    for k in range(3):
        w1t[pl.ds(k * C, C), :] = w1_ref[k].T
        w2t[pl.ds(k * C, C), :] = w2_ref[k].T


def first_layer(me, nb, early, late, xe, w1_ref, pw, hs_a, hs_b, u_s, s_s, z1e):
    n1, Q, C = z1e.shape
    L = n1 - 2 * HZ
    H = C // 2
    b1 = min(8, n1)
    steps = (n1 + b1 - 1) // b1
    edge = min((HX + L - 2 * D1) // b1, steps - 1)

    def chunk(at):
        return jnp.minimum(lax.rem(at + 1, steps) * b1, n1 - b1)

    def mix(at, hs):
        s = chunk(at)
        h = dot(stacked(xe, [s, s + D1, s + 2 * D1], b1), w1_ref[...].reshape(3 * C, C))
        for t in range(2):
            hs[t] = h[:, t * H:(t + 1) * H]

    def activate(at, hs):
        s = chunk(at)
        for t in range(2):
            z = None
            for j in range(4):
                v = hs[t, pl.ds(j, b1 * Q, stride=4), :]
                u, sl = gelu_terms(v)
                u_s[j, pl.ds(s, b1), :, t * H:(t + 1) * H] = u.reshape(b1, Q, H)
                s_s[j, pl.ds(s, b1), :, t * H:(t + 1) * H] = sl.reshape(b1, Q, H)
                term = u * pw[j:j + 1, t * H:(t + 1) * H]
                z = term if z is None else z + term
            z1e[pl.ds(s, b1), :, t * H:(t + 1) * H] = z.reshape(b1, Q, H).astype(BF16)

    mix(0, hs_a)
    pairs = (steps - 1) // 2

    @pl.loop(0, pairs)
    def _(i):
        at = 2 * i

        @pl.when(i == 0)
        def _():
            early()

        @pl.when(i == max((edge - 2) // 2, 0))
        def _():
            late()

        mix(at + 1, hs_b)
        activate(at, hs_a)
        mix(at + 2, hs_a)
        activate(at + 1, hs_b)

    if steps % 2 == 0:
        mix(steps - 1, hs_b)
    activate(2 * pairs, hs_a)
    if steps % 2 == 0:
        activate(steps - 1, hs_b)

    @pl.when(me == 0)
    def _():
        z1e[pl.ds(0, HZ)] = jnp.zeros((HZ, Q, C), BF16)

    @pl.when(me == nb - 1)
    def _():
        z1e[pl.ds(HZ + L, HZ)] = jnp.zeros((HZ, Q, C), BF16)


def second_layer(z1e, ce, w2_ref, dh2e, acc2):
    n2, Q, C = ce.shape
    L = n2 - 2 * HC
    b2 = min(16, n2)
    bg = divisor(L, b2)
    steps, gsteps = (n2 + b2 - 1) // b2, L // bg
    acc2[...] = jnp.zeros_like(acc2)

    def delta(i):
        s = jnp.minimum(i * b2, n2 - b2)
        h = dot(stacked(z1e, [s, s + D2, s + 2 * D2], b2), w2_ref[...].reshape(3 * C, C))
        sl = gelu_terms(h)[1]
        d = ce[pl.ds(s, b2)].reshape(b2 * Q, C).astype(F32) * sl
        dh2e[pl.ds(s, b2)] = d.astype(BF16).reshape(b2, Q, C)

    def weight_gradient(i):
        b = i * bg
        d = dh2e[pl.ds(b + HC, bg)].reshape(bg * Q, C)
        acc2[...] += dot_rows(d, stacked(z1e, [b + HZ - D2, b + HZ, b + HZ + D2], bg))

    lead = min(2, steps)
    both = min(steps, gsteps + lead)
    pl.loop(0, lead)(delta)

    @pl.loop(lead, both)
    def _(i):
        weight_gradient(i - lead)
        delta(i)

    pl.loop(both, steps)(delta)
    pl.loop(both - lead, gsteps)(weight_gradient)


def first_delta(me, nb, dh2e, w2t, pw, u_s, s_s, hs, gpa, dh1e, xe, acc1):
    n3, px, C = dh1e.shape
    L = n3 - 2
    Q = px // 4
    H = C // 2
    gpa[...] = jnp.zeros_like(gpa)
    acc1[...] = jnp.zeros_like(acc1)
    b3 = min(8, n3)
    bx = divisor(L, b3)
    steps, gsteps = (n3 + b3 - 1) // b3, L // bx

    def delta(i):
        s = jnp.minimum(i * b3, n3 - b3)
        o = HC - 1
        dz = dot(stacked(dh2e, [s + o + D2, s + o, s + o - D2], b3), w2t[...])
        band = s + lax.broadcasted_iota(jnp.int32, (b3, Q, 1), 0).reshape(b3 * Q, 1)
        own = (band >= jnp.maximum(1, i * b3)) & (band <= L)
        dzo = jnp.where(own, dz, 0.0)
        for t in range(2):
            cols = slice(t * H, (t + 1) * H)
            for j in range(4):
                u = u_s[j, pl.ds(s + HZ - 1, b3), :, cols].reshape(b3 * Q, H)
                sl = s_s[j, pl.ds(s + HZ - 1, b3), :, cols].reshape(b3 * Q, H)
                hs[t, pl.ds(j, b3 * Q, stride=4), :] = dz[:, cols] * pw[j:j + 1, cols] * sl
                gpa[j, :, cols] += jnp.sum((dzo[:, cols] * u).reshape(-1, 8, H), axis=0)
        for t in range(2):
            cols = slice(t * H, (t + 1) * H)
            dh1e[pl.ds(s, b3), :, cols] = hs[t].astype(BF16).reshape(b3, px, H)

    def weight_gradient(i):
        b = i * bx
        d = dh1e[pl.ds(b + 1, bx)].reshape(bx * px, C)
        acc1[...] += dot_rows(d, stacked(xe, [b + HX - D1, b + HX, b + HX + D1], bx))

    lead = min(2, steps)
    both = min(steps, gsteps + lead)
    pl.loop(0, lead)(delta)

    @pl.loop(lead, both)
    def _(i):
        weight_gradient(i - lead)
        delta(i)

    pl.loop(both, steps)(delta)

    @pl.when(me == 0)
    def _():
        dh1e[0] = jnp.zeros((px, C), BF16)

    @pl.when(me == nb - 1)
    def _():
        dh1e[L + 1] = jnp.zeros((px, C), BF16)

    pl.loop(both - lead, gsteps)(weight_gradient)


def input_gradient(dh1e, w1t, dx_ref, hooks, finish):
    L, px, C = dx_ref.shape
    bx = divisor(L, 8)
    steps = L // bx

    @pl.loop(0, steps)
    def _(i):
        for at, hook in hooks:
            pl.when(i == min(at, steps - 1))(hook)
        b = i * bx
        g = dot(stacked(dh1e, [b + 1 + D1, b + 1, b + 1 - D1], bx), w1t[...])
        dx_ref[pl.ds(b, bx)] = g.astype(BF16).reshape(bx, px, C)
        finish(pl.ds(b, bx))


def local_kernel(
    nb,
    x_hbm, xlo_hbm, xhi_hbm, cot_hbm, clo_hbm, chi_hbm, w1_ref, w2_ref, pw_ref,
    dx_ref, g_ref, gp_ref,
    xe, ce, z1e, dh2e, dh1e, u_s, s_s, hs, hs_b, w1t, w2t, acc1, acc2, gpa, sems,
):
    L, px, C = x_hbm.shape
    me = lax.axis_index("band")
    copies = copy_in([
        (xlo_hbm, xe.at[pl.ds(0, HX)]),
        (x_hbm, xe.at[pl.ds(HX, L)]),
        (xhi_hbm, xe.at[pl.ds(HX + L, HX)]),
        (clo_hbm, ce.at[pl.ds(0, HC)]),
        (cot_hbm, ce.at[pl.ds(HC, L)]),
        (chi_hbm, ce.at[pl.ds(HC + L, HC)]),
    ], sems)
    turn_weights(w1_ref, w2_ref, w1t, w2t)
    for c in copies:
        c.wait()
    pw = pw_ref[...]
    nothing = lambda *_: None
    first_layer(me, nb, nothing, nothing, xe, w1_ref, pw, hs, hs_b, u_s, s_s, z1e)
    second_layer(z1e, ce, w2_ref, dh2e, acc2)
    first_delta(me, nb, dh2e, w2t, pw, u_s, s_s, hs, gpa, dh1e, xe, acc1)
    input_gradient(dh1e, w1t, dx_ref, [], nothing)
    g_ref[0] = acc1[...].astype(BF16)
    g_ref[1] = acc2[...].astype(BF16)
    gp_ref[...] = jnp.sum(gpa[...], axis=1)


def local_scratch(L, px, C):
    Q = px // 4
    return [
        pltpu.VMEM((L + 2 * HX, px, C), BF16),
        pltpu.VMEM((L + 2 * HC, Q, C), BF16),
        pltpu.VMEM((L + 2 * HZ, Q, C), BF16),
        pltpu.VMEM((L + 2 * HC, Q, C), BF16),
        pltpu.VMEM((L + 2, px, C), BF16),
        pltpu.VMEM((4, L + 2 * HZ, Q, C), F32),
        pltpu.VMEM((4, L + 2 * HZ, Q, C), F32),
        pltpu.VMEM((2, 8 * px, C // 2), F32),
        pltpu.VMEM((2, 8 * px, C // 2), F32),
        pltpu.VMEM((3 * C, C), BF16),
        pltpu.VMEM((3 * C, C), BF16),
        pltpu.VMEM((C, 3 * C), F32),
        pltpu.VMEM((C, 3 * C), F32),
        pltpu.VMEM((4, 8, C), F32),
        pltpu.SemaphoreType.DMA((6,)),
    ]


def local_pass(nb, x, xlo, xhi, cot, clo, chi, w1, w2, pw):
    L, px, C = x.shape
    Q = px // 4
    any_spec = pl.BlockSpec(memory_space=pl.ANY)
    vm = pl.BlockSpec(memory_space=pltpu.VMEM)
    return pl.pallas_call(
        functools.partial(local_kernel, nb),
        out_shape=(
            jax.ShapeDtypeStruct((L, px, C), BF16),
            jax.ShapeDtypeStruct((2, C, 3 * C), BF16),
            jax.ShapeDtypeStruct((4, C), F32),
        ),
        in_specs=[any_spec] * 6 + [vm] * 3,
        out_specs=[vm] * 3,
        scratch_shapes=local_scratch(L, px, C),
        compiler_params=pltpu.CompilerParams(vmem_limit_bytes=60 * 1024 * 1024),
        name="local_pass",
    )(x, xlo, xhi, cot, clo, chi, w1, w2, pw)


def blocks(n, count):
    size = -(-n // count)
    return size, [min(i * size, n - size) for i in range(count)]


def inner_first(starts, size, n, rim):
    inner = [s for s in starts if s >= rim and s + size <= n - rim]
    outer = [s for s in starts if s not in inner]
    return inner, sorted(outer, reverse=True)


def fresh(starts, size, taps, low, high):
    seen, pieces = set(), []
    for s in starts:
        rows = [r for r in range(max(s, low), min(s + size + taps, high)) if r not in seen]
        seen.update(rows)
        runs = []
        for r in rows:
            if runs and runs[-1][0] + runs[-1][1] == r:
                runs[-1][1] += 1
            else:
                runs.append([r, 1])
        pieces.append([tuple(run) for run in runs])
    rest = [r for r in range(low, high) if r not in seen]
    assert not rest
    return pieces


def first_plan(L):
    n1 = L + 2 * HZ
    size, starts = blocks(n1, min(6, n1))
    inner, outer = inner_first(starts, size, n1, HZ)
    order = inner + outer
    return n1, size, order, len(inner), fresh(order, size, 2 * D1, HX, HX + L)


def step_kernel(
    scale, lo_n, hi_n,
    x_hbm, cot_hbm, w1_hbm, w2_hbm, pw_ref,
    dx_ref, o_ref, op_ref,
    xe, ce, z1e, dh2e, dh1e, dt, u_s, s_s, hs_a, hs_b, h2_a, h2_b, dz_a, dz_b,
    w1, w2, w1t, w2t, gpa, xsem, sems,
    big, tap, p0, p1, p2, q0, hsend, hrecv, ssem, rsem, spare,
):
    L, px, C = x_hbm.shape
    Q = px // 4
    H = C // 2
    R = C // (lo_n * hi_n)
    dp = lax.axis_index("dp")
    core = lax.axis_index("band")
    other = 1 - core
    lo, hi = lax.rem(dp, lo_n), dp // lo_n
    planes = [hi * lo_n + lax.rem(lo + m, lo_n) for m in range(1, lo_n)]
    lines = [lax.rem(hi + m, hi_n) * lo_n + lo for m in range(1, hi_n)]
    partner = (dp, other)

    barrier = pltpu.get_barrier_semaphore()
    targets = [partner] + [(d, core) for d in planes] + [(d, c) for d in lines for c in (core, other)]
    for t in targets:
        pl.semaphore_signal(barrier, inc=1, device_id=t, device_id_type=MESH)

    n1, b1, order1, inner1, pieces = first_plan(L)
    first = pltpu.make_async_copy(w1_hbm, w1, sems.at[0])
    first.start()
    loads, at = [], 0
    for runs in pieces:
        mine = []
        for r, n in runs:
            c = pltpu.make_async_copy(x_hbm.at[pl.ds(r - HX, n)], xe.at[pl.ds(r, n)], xsem.at[at])
            c.start()
            mine.append(c)
            at += 1
        loads.append(mine)
    second = [pltpu.make_async_copy(w2_hbm, w2, sems.at[1]),
              pltpu.make_async_copy(cot_hbm, ce.at[pl.ds(HC, L)], sems.at[2])]
    for c in second:
        c.start()
    xpad = jnp.where(core == 0, 0, HX + L)
    cpad = jnp.where(core == 0, 0, HC + L)
    xe[pl.ds(xpad, HX)] = jnp.zeros((HX, px, C), BF16)
    ce[pl.ds(cpad, HC)] = jnp.zeros((HC, Q, C), BF16)
    gpa[...] = jnp.zeros_like(gpa)
    pw = pw_ref[...]
    pwb = pw.astype(BF16)

    def halos():
        return [
            pltpu.make_async_remote_copy(
                src_ref=src.at[pl.ds(jnp.where(core == 0, L - w, 0), w)],
                dst_ref=dst.at[pl.ds(jnp.where(core == 0, 0, w + L), w)],
                send_sem=hsend.at[i], recv_sem=hrecv.at[i],
                device_id=partner, device_id_type=MESH,
            )
            for i, (src, dst, w) in enumerate([(x_hbm, xe, HX), (cot_hbm, ce, HC)])
        ]

    def link(i, src, dst, target):
        return pltpu.make_async_remote_copy(
            src_ref=src, dst_ref=dst, send_sem=ssem.at[i], recv_sem=rsem.at[i],
            device_id=target, device_id_type=MESH,
        )

    per = 1 + (lo_n - 1) + 2 * (hi_n - 1) + 1

    def start(cs):
        for c in cs:
            c.start()

    def arrived(cs):
        for c in cs:
            c.wait_recv()

    def reducer(slot, refs):
        gb, r0, s0, r1, s1, r2 = refs
        base = slot * per

        def across():
            return [link(base, gb.at[other], r0, partner)]

        def plane():
            return [link(base + 1 + m, s0.at[m], r1.at[m], (planes[m], core))
                    for m in range(lo_n - 1)]

        def line():
            out = []
            for m in sorted(range(hi_n - 1), key=lambda m: abs(m + 1 - hi_n / 2)):
                src = s1.at[lax.rem(hi + m + 1, hi_n)]
                for k, c in enumerate((core, other)):
                    out.append(link(base + lo_n + 2 * m + k, src, r2.at[k, m], (lines[m], c)))
            out.append(link(base + per - 1, s1.at[hi], r2.at[1, hi_n - 1], partner))
            return out

        def step_a(parts):
            for h in range(2):
                for k, part in enumerate(parts):
                    rows = part[:, h * H:(h + 1) * H].astype(BF16).reshape(hi_n, lo_n, R, H)
                    for l in range(lo_n):
                        gb[h, l, :, :, k * H:(k + 1) * H] = rows[:, l]
            start(across())

        def step_b():
            arrived(across())
            out = plane()
            for m in range(lo_n - 1):
                at = lax.rem(lo + m + 1, lo_n)
                s0[m] = (gb[core, at].astype(F32) + r0[at].astype(F32)).astype(BF16)
                out[m].start()

        def step_c():
            arrived(plane())
            own = gb[core, lo].astype(F32) + r0[lo].astype(F32)
            for m in range(lo_n - 1):
                own = own + r1[m].astype(F32)
            s1[...] = own.astype(BF16)
            start(line())

        def step_d(put):
            arrived(line())
            mine = s1[hi].astype(F32)
            theirs = r2[1, hi_n - 1].astype(F32)
            for m in range(hi_n - 1):
                mine = mine + r2[0, m].astype(F32)
                theirs = theirs + r2[1, m].astype(F32)
            a = jnp.where(core == 0, mine, theirs) * scale
            b = jnp.where(core == 0, theirs, mine) * scale
            for k in range(a.shape[-1] // H):
                put(k, jnp.concatenate([a[:, k * H:(k + 1) * H], b[:, k * H:(k + 1) * H]], axis=-1))

        return step_a, step_b, step_c, step_d, lambda: across() + plane() + line()

    second_sum = reducer(0, big)
    tap_sums = [reducer(1 + k, [r.at[k] for r in tap]) for k in range(3)]
    pbase = 4 * per

    def pairs_p():
        return [link(pbase, q0.at[0], p0, partner)]

    def plane_p():
        return [link(pbase + 1 + m, q0.at[1], p1.at[lo], (planes[m], core)) for m in range(lo_n - 1)]

    def line_p():
        return [link(pbase + lo_n + m, q0.at[2], p2.at[hi], (lines[m], core)) for m in range(hi_n - 1)]

    def patch_a():
        q0[0] = jnp.sum(gpa[...], axis=1)
        start(pairs_p())

    def patch_b():
        arrived(pairs_p())
        q0[1] = q0[0] + p0[...]
        p1[lo] = q0[0] + p0[...]
        start(plane_p())

    def patch_c():
        arrived(plane_p())
        total = jnp.sum(p1[...], axis=0)
        q0[2] = total
        p2[hi] = total
        start(line_p())

    def patch_d():
        arrived(line_p())
        op_ref[...] = jnp.sum(p2[...], axis=0) * scale

    def mix(i, hs):
        s = order1[i]
        for c in loads[i]:
            c.wait()
        h = dot(stacked(xe, [s, s + D1, s + 2 * D1], b1), w1[...].reshape(3 * C, C))
        for t in range(2):
            hs[t, :b1 * px] = h[:, t * H:(t + 1) * H]

    def activate(i, hs):
        s = order1[i]
        g = divisor(b1, 8)
        for r in range(0, b1, g):
            for t in range(2):
                cols = slice(t * H, (t + 1) * H)
                z = None
                for j in range(4):
                    v = hs[t, pl.ds(r * px + j, g * Q, stride=4), :].astype(BF16)
                    u, sl = gelu_terms(v)
                    u_s[j, s + r:s + r + g, :, cols] = u.astype(u_s.dtype).reshape(g, Q, H)
                    s_s[j, s + r:s + r + g, :, cols] = sl.astype(s_s.dtype).reshape(g, Q, H)
                    term = (u * pwb[j:j + 1, cols]).astype(F32)
                    z = term if z is None else z + term
                z1e[s + r:s + r + g, :, cols] = z.reshape(g, Q, H).astype(BF16)

    n2 = L + 2 * HC
    b2, starts2 = blocks(n2, min(3, n2))
    order2 = sum(inner_first(starts2, b2, n2, HC), [])

    def mix2(i, h2):
        s = order2[i]
        h2[...] = dot(stacked(z1e, [s, s + D2, s + 2 * D2], b2), w2[...].reshape(3 * C, C))

    def activate2(i, h2):
        s = order2[i]
        g = divisor(b2, 8)
        for r in range(0, b2, g):
            sl = gelu_terms(h2[r * Q:(r + g) * Q, :])[1]
            d = ce[s + r:s + r + g].reshape(g * Q, C).astype(F32) * sl
            dh2e[s + r:s + r + g] = d.astype(BF16).reshape(g, Q, C)

    n3 = L + 2
    b3, order3 = blocks(n3, min(3, n3))

    def mix3(i, dz):
        s = order3[i] + HC - 1
        dz[...] = dot(stacked(dh2e, [s + D2, s, s - D2], b3), w2t[...])

    def delta(i, dz, hs):
        s = order3[i]
        done = 0 if i == 0 else order3[i - 1] + b3
        g = divisor(b3, 8)
        for r in range(0, b3, g):
            own = [b for b in range(s + r, s + r + g) if 1 <= b <= L and b >= done]
            for t in range(2):
                cols = slice(t * H, (t + 1) * H)
                d = dz[r * Q:(r + g) * Q, cols].astype(BF16)
                for j in range(4):
                    where = slice(s + r + HZ - 1, s + r + g + HZ - 1)
                    u = u_s[j, where, :, cols].reshape(g * Q, H)
                    sl = s_s[j, where, :, cols].reshape(g * Q, H)
                    hs[t, pl.ds(r * px + j, g * Q, stride=4), :] = (
                        d * pwb[j:j + 1, cols] * sl).astype(F32)
                    if own:
                        a, b = (own[0] - s - r) * Q, (own[-1] + 1 - s - r) * Q
                        m = (d[a:b] * u[a:b]).reshape(len(own), Q, H)
                        part = m[0]
                        for k in range(1, len(own)):
                            part = part + m[k]
                        gpa[j, :, cols] += part.astype(F32)
            for t in range(2):
                cols = slice(t * H, (t + 1) * H)
                dh1e[s + r:s + r + g, :, cols] = (
                    hs[t, r * px:(r + g) * px].astype(BF16).reshape(g, px, H))

    bt = max(b for b in range(1, min(L, 16) + 1) if L % b == 0 and b * px % 128 == 0)

    def turn(upto):
        while turned[0] < L // bt and (turned[0] + 1) * bt + 1 <= upto:
            i = turned[0]
            dt[:, i * bt * px:(i + 1) * bt * px] = dh1e[1 + i * bt:1 + (i + 1) * bt].reshape(bt * px, C).T
            turned[0] += 1

    turned = [0]

    def first_gradient(k):
        x = xe[pl.ds(HX + (k - 1) * D1, L)].reshape(L * px, C)
        tap_sums[k][0]([dot(dt[...], x)])

    def input_gradient_of(b, n):
        g = dot(stacked(dh1e, [b + 1 + D1, b + 1, b + 1 - D1], n), w1t[...])
        dx_ref[pl.ds(b, n)] = g.astype(BF16).reshape(n, px, C)

    first.wait()
    steps = len(order1)
    hs = [hs_a, hs_b]
    for i in range(steps + 1):
        if i < steps:
            if i == inner1:
                for c in halos():
                    c.wait()
            mix(i, hs[i % 2])
        if i == 0:
            pl.semaphore_wait(barrier, len(targets))
            for c in halos():
                c.start()
        if i == 2:
            for c in second:
                c.wait()
            turn_weights(w1, w2, w1t, w2t)
        if i:
            activate(i - 1, hs[(i - 1) % 2])

    @pl.when(core == 0)
    def _():
        z1e[pl.ds(0, HZ)] = jnp.zeros((HZ, Q, C), BF16)

    @pl.when(core == 1)
    def _():
        z1e[pl.ds(HZ + L, HZ)] = jnp.zeros((HZ, Q, C), BF16)

    h2 = [h2_a, h2_b]
    for i in range(len(order2) + 1):
        if i < len(order2):
            mix2(i, h2[i % 2])
        if i:
            activate2(i - 1, h2[(i - 1) % 2])

    dz = [dz_a, dz_b]
    mix3(0, dz[0])
    d2 = dh2e[pl.ds(HC, L)].reshape(L * Q, C)
    acc2 = dot_rows(d2, stacked(z1e, [HZ - D2, HZ, HZ + D2], L))
    second_sum[0]([acc2[:, k * C:(k + 1) * C] for k in range(3)])
    count = len(order3)
    for i in range(count):
        if i + 1 < count:
            mix3(i + 1, dz[(i + 1) % 2])
        delta(i, dz[i % 2], hs[i % 2])
        if i + 1 < count:
            turn(order3[i] + b3)
        if i == count - 2:
            second_sum[1]()

    patch_a()

    @pl.when(core == 0)
    def _():
        dh1e[0] = jnp.zeros((px, C), BF16)

    @pl.when(core == 1)
    def _():
        dh1e[L + 1] = jnp.zeros((px, C), BF16)

    turn(n3)
    first_gradient(0)
    first_gradient(1)
    patch_b()
    first_gradient(2)
    tap_sums[0][1]()
    pieces4 = 4 if L % 4 == 0 else 1
    n = L // pieces4
    after = [
        [tap_sums[1][1]],
        [tap_sums[2][1]],
        [second_sum[2], patch_c],
        [],
    ]

    def put2(k, row):
        o_ref[1, k] = row

    def put1(tap_index):
        def put(k, row):
            o_ref[0, tap_index] = row
        return put

    for i in range(pieces4):
        input_gradient_of(i * n, n)
        for hook in (after[i] if pieces4 == 4 else sum(after, [])):
            hook()
    tap_sums[0][2]()
    tap_sums[1][2]()
    tap_sums[2][2]()
    patch_d()
    second_sum[3](put2)
    for k in range(3):
        tap_sums[k][3](put1(k))
    for part in [second_sum] + tap_sums:
        for c in part[4]():
            c.wait_send()
    for c in pairs_p() + plane_p() + line_p():
        c.wait_send()


def step_pass(scale, ndp, x, cot, w1, w2, pw):
    L, px, C = x.shape
    Q = px // 4
    H = C // 2
    R = C // ndp
    lo_n = divisor(ndp, math.isqrt(ndp))
    hi_n = ndp // lo_n
    n = 4 * (lo_n + 2 * (hi_n - 1) + 1) + lo_n + hi_n - 1
    hbm = pl.BlockSpec(memory_space=pltpu.HBM)
    vm = pl.BlockSpec(memory_space=pltpu.VMEM)
    _, b1, _, _, pieces = first_plan(L)
    b2 = blocks(L + 2 * HC, 3)[0]
    b3 = blocks(L + 2, 3)[0]
    wide = max(b1, b3)

    def sums(lead, w):
        return [
            pltpu.VMEM(lead + (2, lo_n, hi_n, R, w), BF16),
            pltpu.VMEM(lead + (lo_n, hi_n, R, w), BF16),
            pltpu.VMEM(lead + (lo_n - 1, hi_n, R, w), BF16),
            pltpu.VMEM(lead + (lo_n - 1, hi_n, R, w), BF16),
            pltpu.VMEM(lead + (hi_n, R, w), BF16),
            pltpu.VMEM(lead + (2, hi_n, R, w), BF16),
        ]

    limit = 67043328 - (L * px * C * 2 + (1 << 18))
    scratch = [
        pltpu.VMEM((L + 2 * HX, px, C), BF16),
        pltpu.VMEM((L + 2 * HC, Q, C), BF16),
        pltpu.VMEM((L + 2 * HZ, Q, C), BF16),
        pltpu.VMEM((L + 2 * HC, Q, C), BF16),
        pltpu.VMEM((L + 2, px, C), BF16),
        pltpu.VMEM((C, L * px), BF16),
        pltpu.VMEM((4, L + 2 * HZ, Q, C), BF16),
        pltpu.VMEM((4, L + 2 * HZ, Q, C), BF16),
        pltpu.VMEM((2, wide * px, H), F32),
        pltpu.VMEM((2, wide * px, H), F32),
        pltpu.VMEM((b2 * Q, C), F32),
        pltpu.VMEM((b2 * Q, C), F32),
        pltpu.VMEM((b3 * Q, C), F32),
        pltpu.VMEM((b3 * Q, C), F32),
        pltpu.VMEM((3, C, C), BF16),
        pltpu.VMEM((3, C, C), BF16),
        pltpu.VMEM((3 * C, C), BF16),
        pltpu.VMEM((3 * C, C), BF16),
        pltpu.VMEM((4, Q, C), F32),
        pltpu.SemaphoreType.DMA((sum(len(p) for p in pieces),)),
        pltpu.SemaphoreType.DMA((3,)),
        sums((), 3 * H),
        sums((3,), H),
        pltpu.VMEM((4, C), F32),
        pltpu.VMEM((lo_n, 4, C), F32),
        pltpu.VMEM((hi_n, 4, C), F32),
        pltpu.VMEM((3, 4, C), F32),
        pltpu.SemaphoreType.DMA((2,)),
        pltpu.SemaphoreType.DMA((2,)),
        pltpu.SemaphoreType.DMA((n,)),
        pltpu.SemaphoreType.DMA((n,)),
    ]
    used = sum(math.prod(r.shape) * jnp.dtype(r.dtype).itemsize
               for r in jax.tree.leaves(scratch) if r.memory_space == pltpu.VMEM)
    spare = max((limit - used - (1 << 20)) // (8 * 128 * 4), 1) * 128
    return pl.pallas_call(
        functools.partial(step_kernel, scale, lo_n, hi_n),
        out_shape=(
            pltpu.VMEM((L, px, C), BF16),
            pltpu.VMEM((2, 3, R, C), F32),
            pltpu.VMEM((4, C), F32),
        ),
        in_specs=[hbm] * 4 + [vm],
        out_specs=[vm, vm, vm],
        scratch_shapes=scratch + [pltpu.VMEM((8, spare), F32)],
        compiler_params=pltpu.CompilerParams(
            collective_id=0, has_side_effects=True, vmem_limit_bytes=limit
        ),
        name="step_pass",
    )(x, cot, w1, w2, pw)


def hand_over_kernel(n, dx_ref, o_ref, p_ref, dx_out, o1_out, o2_out, p_out, sem):
    step = dx_ref.shape[0] // n
    out = [pltpu.make_async_copy(dx_ref.at[pl.ds(i * step, step)], dx_out.at[pl.ds(i * step, step)],
                                 sem.at[i]) for i in range(n)]
    for c in out:
        c.start()
    o1_out[...] = o_ref[0]
    o2_out[...] = o_ref[1]
    p_out[...] = p_ref[...]
    for c in out:
        c.wait()


def hand_over(dx, o, p):
    n = divisor(dx.shape[0], 4)
    vm = pl.BlockSpec(memory_space=pltpu.VMEM)
    one = jax.ShapeDtypeStruct(o.shape[1:], F32)
    dx, o1, o2, p = pl.pallas_call(
        functools.partial(hand_over_kernel, n),
        out_shape=(jax.ShapeDtypeStruct(dx.shape, dx.dtype), one, one,
                   jax.ShapeDtypeStruct(p.shape, F32)),
        in_specs=[vm, vm, vm],
        out_specs=[pl.BlockSpec(memory_space=pltpu.HBM), vm, vm, vm],
        scratch_shapes=[pltpu.SemaphoreType.DMA((n,))],
        compiler_params=pltpu.CompilerParams(vmem_limit_bytes=16 * 1024 * 1024),
        name="hand_over",
    )(dx, o, p)
    return dx, jnp.transpose(o1, (1, 0, 2)), jnp.transpose(o2, (1, 0, 2)), p


def shards(ndp, nb, x, w1, w2, pw, cot):
    L, px, C = x.shape
    Q = px // 4
    scale = 1.0 / math.sqrt(L * nb * px * ndp)
    if nb == 2 and ndp >= 4 and (C // ndp) % 16 == 0 and C % 256 == 0 and L >= 48 and L * px % 128 == 0:
        return hand_over(*step_pass(scale, ndp, x, cot, w1, w2, pw))
    up = [(i, i + 1) for i in range(nb - 1)]
    down = [(j, i) for i, j in up]

    def edges(x_part, c_part, pairs):
        both = jnp.concatenate([x_part.reshape(HX * px, C), c_part.reshape(HC * Q, C)], axis=0)
        both = lax.ppermute(both, "band", pairs)
        return both[:HX * px].reshape(HX, px, C), both[HX * px:].reshape(HC, Q, C)

    xlo, clo = edges(x[L - HX:], cot[L - HC:], up)
    xhi, chi = edges(x[:HX], cot[:HC], down)
    dx, g, gp = local_pass(nb, x, xlo, xhi, cot, clo, chi, w1, w2, pw)
    kept = lax.psum_scatter(g.astype(F32), "dp", scatter_dimension=1, tiled=True)
    kept = (lax.psum(kept, "band") * scale).reshape(2, C // ndp, 3, C)
    o1, o2 = kept[0], kept[1]
    op = lax.psum(gp, ("dp", "band")) * scale
    return dx, o1, o2, op


def solution(mesh):
    placed = (P("band", "dp", None), P(), P(), P(), P("band", "dp", None))
    return jax.shard_map(
        functools.partial(shards, mesh.shape["dp"], mesh.shape["band"]),
        mesh=mesh,
        in_specs=placed,
        out_specs=(P("band", "dp", None), P("dp", None, None), P("dp", None, None), P()),
        check_vma=False,
    )
```

```python
import functools
import math

import jax
import jax.numpy as jnp
from jax import lax
from jax.experimental import pallas as pl
from jax.experimental.pallas import tpu as pltpu
from jax.sharding import PartitionSpec as P

D1 = 1
D2 = 2
HZ = 1 + 2 * D2
HX = HZ + D1
HC = 1 + D2
MESH = pl.DeviceIdType.MESH
F32 = jnp.float32
BF16 = jnp.bfloat16
G0 = math.sqrt(2.0 / math.pi)
G1 = 0.044715 * G0


def divisor(n, most):
    return max(i for i in range(1, min(n, most) + 1) if n % i == 0)


def gelu_terms(v):
    sq = v * v
    p = 0.5 + 0.5 * jnp.tanh(v * (G0 + G1 * sq))
    u = v * p
    s = p + u * (1.0 - p) * (2.0 * G0 + (6.0 * G1) * sq)
    return u, s


def dot(a, b):
    return jnp.dot(a, b, preferred_element_type=F32)


def dot_rows(a, b):
    return lax.dot_general(a, b, (((0,), (0,)), ((), ())), preferred_element_type=F32)


def stacked(ref, starts, n):
    c = ref.shape[-1]
    return jnp.concatenate([ref[pl.ds(s, n)].reshape(-1, c) for s in starts], axis=-1)


def copy_in(pairs, sems):
    copies = [pltpu.make_async_copy(a, b, sems.at[i]) for i, (a, b) in enumerate(pairs)]
    for c in copies:
        c.start()
    return copies


def turn_weights(w1_ref, w2_ref, w1t, w2t):
    C = w1_ref.shape[-1]
    for k in range(3):
        w1t[pl.ds(k * C, C), :] = w1_ref[k].T
        w2t[pl.ds(k * C, C), :] = w2_ref[k].T


def first_layer(me, nb, early, late, xe, w1_ref, pw, hs_a, hs_b, u_s, s_s, z1e):
    n1, Q, C = z1e.shape
    L = n1 - 2 * HZ
    H = C // 2
    b1 = min(8, n1)
    steps = (n1 + b1 - 1) // b1
    edge = min((HX + L - 2 * D1) // b1, steps - 1)

    def chunk(at):
        return jnp.minimum(lax.rem(at + 1, steps) * b1, n1 - b1)

    def mix(at, hs):
        s = chunk(at)
        h = dot(stacked(xe, [s, s + D1, s + 2 * D1], b1), w1_ref[...].reshape(3 * C, C))
        for t in range(2):
            hs[t] = h[:, t * H:(t + 1) * H]

    def activate(at, hs):
        s = chunk(at)
        for t in range(2):
            z = None
            for j in range(4):
                v = hs[t, pl.ds(j, b1 * Q, stride=4), :]
                u, sl = gelu_terms(v)
                u_s[j, pl.ds(s, b1), :, t * H:(t + 1) * H] = u.reshape(b1, Q, H)
                s_s[j, pl.ds(s, b1), :, t * H:(t + 1) * H] = sl.reshape(b1, Q, H)
                term = u * pw[j:j + 1, t * H:(t + 1) * H]
                z = term if z is None else z + term
            z1e[pl.ds(s, b1), :, t * H:(t + 1) * H] = z.reshape(b1, Q, H).astype(BF16)

    mix(0, hs_a)
    pairs = (steps - 1) // 2

    @pl.loop(0, pairs)
    def _(i):
        at = 2 * i

        @pl.when(i == 0)
        def _():
            early()

        @pl.when(i == max((edge - 2) // 2, 0))
        def _():
            late()

        mix(at + 1, hs_b)
        activate(at, hs_a)
        mix(at + 2, hs_a)
        activate(at + 1, hs_b)

    if steps % 2 == 0:
        mix(steps - 1, hs_b)
    activate(2 * pairs, hs_a)
    if steps % 2 == 0:
        activate(steps - 1, hs_b)

    @pl.when(me == 0)
    def _():
        z1e[pl.ds(0, HZ)] = jnp.zeros((HZ, Q, C), BF16)

    @pl.when(me == nb - 1)
    def _():
        z1e[pl.ds(HZ + L, HZ)] = jnp.zeros((HZ, Q, C), BF16)


def second_layer(z1e, ce, w2_ref, dh2e, acc2):
    n2, Q, C = ce.shape
    L = n2 - 2 * HC
    b2 = min(16, n2)
    bg = divisor(L, b2)
    steps, gsteps = (n2 + b2 - 1) // b2, L // bg
    acc2[...] = jnp.zeros_like(acc2)

    def delta(i):
        s = jnp.minimum(i * b2, n2 - b2)
        h = dot(stacked(z1e, [s, s + D2, s + 2 * D2], b2), w2_ref[...].reshape(3 * C, C))
        sl = gelu_terms(h)[1]
        d = ce[pl.ds(s, b2)].reshape(b2 * Q, C).astype(F32) * sl
        dh2e[pl.ds(s, b2)] = d.astype(BF16).reshape(b2, Q, C)

    def weight_gradient(i):
        b = i * bg
        d = dh2e[pl.ds(b + HC, bg)].reshape(bg * Q, C)
        acc2[...] += dot_rows(d, stacked(z1e, [b + HZ - D2, b + HZ, b + HZ + D2], bg))

    lead = min(2, steps)
    both = min(steps, gsteps + lead)
    pl.loop(0, lead)(delta)

    @pl.loop(lead, both)
    def _(i):
        weight_gradient(i - lead)
        delta(i)

    pl.loop(both, steps)(delta)
    pl.loop(both - lead, gsteps)(weight_gradient)


def first_delta(me, nb, dh2e, w2t, pw, u_s, s_s, hs, gpa, dh1e, xe, acc1):
    n3, px, C = dh1e.shape
    L = n3 - 2
    Q = px // 4
    H = C // 2
    gpa[...] = jnp.zeros_like(gpa)
    acc1[...] = jnp.zeros_like(acc1)
    b3 = min(8, n3)
    bx = divisor(L, b3)
    steps, gsteps = (n3 + b3 - 1) // b3, L // bx

    def delta(i):
        s = jnp.minimum(i * b3, n3 - b3)
        o = HC - 1
        dz = dot(stacked(dh2e, [s + o + D2, s + o, s + o - D2], b3), w2t[...])
        band = s + lax.broadcasted_iota(jnp.int32, (b3, Q, 1), 0).reshape(b3 * Q, 1)
        own = (band >= jnp.maximum(1, i * b3)) & (band <= L)
        dzo = jnp.where(own, dz, 0.0)
        for t in range(2):
            cols = slice(t * H, (t + 1) * H)
            for j in range(4):
                u = u_s[j, pl.ds(s + HZ - 1, b3), :, cols].reshape(b3 * Q, H)
                sl = s_s[j, pl.ds(s + HZ - 1, b3), :, cols].reshape(b3 * Q, H)
                hs[t, pl.ds(j, b3 * Q, stride=4), :] = dz[:, cols] * pw[j:j + 1, cols] * sl
                gpa[j, :, cols] += jnp.sum((dzo[:, cols] * u).reshape(-1, 8, H), axis=0)
        for t in range(2):
            cols = slice(t * H, (t + 1) * H)
            dh1e[pl.ds(s, b3), :, cols] = hs[t].astype(BF16).reshape(b3, px, H)

    def weight_gradient(i):
        b = i * bx
        d = dh1e[pl.ds(b + 1, bx)].reshape(bx * px, C)
        acc1[...] += dot_rows(d, stacked(xe, [b + HX - D1, b + HX, b + HX + D1], bx))

    lead = min(2, steps)
    both = min(steps, gsteps + lead)
    pl.loop(0, lead)(delta)

    @pl.loop(lead, both)
    def _(i):
        weight_gradient(i - lead)
        delta(i)

    pl.loop(both, steps)(delta)

    @pl.when(me == 0)
    def _():
        dh1e[0] = jnp.zeros((px, C), BF16)

    @pl.when(me == nb - 1)
    def _():
        dh1e[L + 1] = jnp.zeros((px, C), BF16)

    pl.loop(both - lead, gsteps)(weight_gradient)


def input_gradient(dh1e, w1t, dx_ref, hooks, finish):
    L, px, C = dx_ref.shape
    bx = divisor(L, 8)
    steps = L // bx

    @pl.loop(0, steps)
    def _(i):
        for at, hook in hooks:
            pl.when(i == min(at, steps - 1))(hook)
        b = i * bx
        g = dot(stacked(dh1e, [b + 1 + D1, b + 1, b + 1 - D1], bx), w1t[...])
        dx_ref[pl.ds(b, bx)] = g.astype(BF16).reshape(bx, px, C)
        finish(pl.ds(b, bx))


def local_kernel(
    nb,
    x_hbm, xlo_hbm, xhi_hbm, cot_hbm, clo_hbm, chi_hbm, w1_ref, w2_ref, pw_ref,
    dx_ref, g_ref, gp_ref,
    xe, ce, z1e, dh2e, dh1e, u_s, s_s, hs, hs_b, w1t, w2t, acc1, acc2, gpa, sems,
):
    L, px, C = x_hbm.shape
    me = lax.axis_index("band")
    copies = copy_in([
        (xlo_hbm, xe.at[pl.ds(0, HX)]),
        (x_hbm, xe.at[pl.ds(HX, L)]),
        (xhi_hbm, xe.at[pl.ds(HX + L, HX)]),
        (clo_hbm, ce.at[pl.ds(0, HC)]),
        (cot_hbm, ce.at[pl.ds(HC, L)]),
        (chi_hbm, ce.at[pl.ds(HC + L, HC)]),
    ], sems)
    turn_weights(w1_ref, w2_ref, w1t, w2t)
    for c in copies:
        c.wait()
    pw = pw_ref[...]
    nothing = lambda *_: None
    first_layer(me, nb, nothing, nothing, xe, w1_ref, pw, hs, hs_b, u_s, s_s, z1e)
    second_layer(z1e, ce, w2_ref, dh2e, acc2)
    first_delta(me, nb, dh2e, w2t, pw, u_s, s_s, hs, gpa, dh1e, xe, acc1)
    input_gradient(dh1e, w1t, dx_ref, [], nothing)
    g_ref[0] = acc1[...].astype(BF16)
    g_ref[1] = acc2[...].astype(BF16)
    gp_ref[...] = jnp.sum(gpa[...], axis=1)


def local_scratch(L, px, C):
    Q = px // 4
    return [
        pltpu.VMEM((L + 2 * HX, px, C), BF16),
        pltpu.VMEM((L + 2 * HC, Q, C), BF16),
        pltpu.VMEM((L + 2 * HZ, Q, C), BF16),
        pltpu.VMEM((L + 2 * HC, Q, C), BF16),
        pltpu.VMEM((L + 2, px, C), BF16),
        pltpu.VMEM((4, L + 2 * HZ, Q, C), F32),
        pltpu.VMEM((4, L + 2 * HZ, Q, C), F32),
        pltpu.VMEM((2, 8 * px, C // 2), F32),
        pltpu.VMEM((2, 8 * px, C // 2), F32),
        pltpu.VMEM((3 * C, C), BF16),
        pltpu.VMEM((3 * C, C), BF16),
        pltpu.VMEM((C, 3 * C), F32),
        pltpu.VMEM((C, 3 * C), F32),
        pltpu.VMEM((4, 8, C), F32),
        pltpu.SemaphoreType.DMA((6,)),
    ]


def local_pass(nb, x, xlo, xhi, cot, clo, chi, w1, w2, pw):
    L, px, C = x.shape
    Q = px // 4
    any_spec = pl.BlockSpec(memory_space=pl.ANY)
    vm = pl.BlockSpec(memory_space=pltpu.VMEM)
    return pl.pallas_call(
        functools.partial(local_kernel, nb),
        out_shape=(
            jax.ShapeDtypeStruct((L, px, C), BF16),
            jax.ShapeDtypeStruct((2, C, 3 * C), BF16),
            jax.ShapeDtypeStruct((4, C), F32),
        ),
        in_specs=[any_spec] * 6 + [vm] * 3,
        out_specs=[vm] * 3,
        scratch_shapes=local_scratch(L, px, C),
        compiler_params=pltpu.CompilerParams(vmem_limit_bytes=60 * 1024 * 1024),
        name="local_pass",
    )(x, xlo, xhi, cot, clo, chi, w1, w2, pw)


def blocks(n, count):
    size = -(-n // count)
    return size, [min(i * size, n - size) for i in range(count)]


def inner_first(starts, size, n, rim):
    inner = [s for s in starts if s >= rim and s + size <= n - rim]
    outer = [s for s in starts if s not in inner]
    return inner, sorted(outer, reverse=True)


def fresh(starts, size, taps, low, high):
    seen, pieces = set(), []
    for s in starts:
        rows = [r for r in range(max(s, low), min(s + size + taps, high)) if r not in seen]
        seen.update(rows)
        runs = []
        for r in rows:
            if runs and runs[-1][0] + runs[-1][1] == r:
                runs[-1][1] += 1
            else:
                runs.append([r, 1])
        pieces.append([tuple(run) for run in runs])
    rest = [r for r in range(low, high) if r not in seen]
    assert not rest
    return pieces


def first_plan(L):
    n1 = L + 2 * HZ
    size, starts = blocks(n1, min(6, n1))
    inner, outer = inner_first(starts, size, n1, HZ)
    order = inner + outer
    return n1, size, order, len(inner), fresh(order, size, 2 * D1, HX, HX + L)


def step_kernel(
    scale, lo_n, hi_n,
    x_hbm, cot_hbm, w1_hbm, w2_hbm, pw_ref,
    dx_ref, o_ref, op_ref,
    xe, ce, z1e, dh2e, dh1e, dt, u_s, s_s, hs_a, hs_b, h2_a, h2_b, dz_a, dz_b,
    w1, w2, w1t, w2t, gpa, xsem, sems,
    big, tap, acc1, p0, p1, p2, q0, hsend, hrecv, ssem, rsem, spare,
):
    L, px, C = x_hbm.shape
    Q = px // 4
    H = C // 2
    R = C // (lo_n * hi_n)
    dp = lax.axis_index("dp")
    core = lax.axis_index("band")
    other = 1 - core
    lo, hi = lax.rem(dp, lo_n), dp // lo_n
    planes = [hi * lo_n + lax.rem(lo + m, lo_n) for m in range(1, lo_n)]
    lines = [lax.rem(hi + m, hi_n) * lo_n + lo for m in range(1, hi_n)]
    partner = (dp, other)

    barrier = pltpu.get_barrier_semaphore()
    targets = [partner] + [(d, core) for d in planes] + [(d, c) for d in lines for c in (core, other)]
    for t in targets:
        pl.semaphore_signal(barrier, inc=1, device_id=t, device_id_type=MESH)

    n1, b1, order1, inner1, pieces = first_plan(L)
    first = pltpu.make_async_copy(w1_hbm, w1, sems.at[0])
    first.start()
    loads, at = [], 0
    for runs in pieces:
        mine = []
        for r, n in runs:
            c = pltpu.make_async_copy(x_hbm.at[pl.ds(r - HX, n)], xe.at[pl.ds(r, n)], xsem.at[at])
            c.start()
            mine.append(c)
            at += 1
        loads.append(mine)
    second = [pltpu.make_async_copy(w2_hbm, w2, sems.at[1]),
              pltpu.make_async_copy(cot_hbm, ce.at[pl.ds(HC, L)], sems.at[2])]
    for c in second:
        c.start()
    xpad = jnp.where(core == 0, 0, HX + L)
    cpad = jnp.where(core == 0, 0, HC + L)
    xe[pl.ds(xpad, HX)] = jnp.zeros((HX, px, C), BF16)
    ce[pl.ds(cpad, HC)] = jnp.zeros((HC, Q, C), BF16)
    gpa[...] = jnp.zeros_like(gpa)
    pw = pw_ref[...]
    pwb = pw.astype(BF16)

    def halos():
        return [
            pltpu.make_async_remote_copy(
                src_ref=src.at[pl.ds(jnp.where(core == 0, L - w, 0), w)],
                dst_ref=dst.at[pl.ds(jnp.where(core == 0, 0, w + L), w)],
                send_sem=hsend.at[i], recv_sem=hrecv.at[i],
                device_id=partner, device_id_type=MESH,
            )
            for i, (src, dst, w) in enumerate([(x_hbm, xe, HX), (cot_hbm, ce, HC)])
        ]

    def link(i, src, dst, target):
        return pltpu.make_async_remote_copy(
            src_ref=src, dst_ref=dst, send_sem=ssem.at[i], recv_sem=rsem.at[i],
            device_id=target, device_id_type=MESH,
        )

    per = 1 + (lo_n - 1) + 2 * (hi_n - 1) + 1

    def start(cs):
        for c in cs:
            c.start()

    def arrived(cs):
        for c in cs:
            c.wait_recv()

    def reducer(slot, refs):
        gb, r0, s0, r1, s1, r2 = refs
        base = slot * per

        def across():
            return [link(base, gb.at[other], r0, partner)]

        def plane():
            return [link(base + 1 + m, s0.at[m], r1.at[m], (planes[m], core))
                    for m in range(lo_n - 1)]

        def line():
            out = []
            for m in sorted(range(hi_n - 1), key=lambda m: abs(m + 1 - hi_n / 2)):
                src = s1.at[lax.rem(hi + m + 1, hi_n)]
                for k, c in enumerate((core, other)):
                    out.append(link(base + lo_n + 2 * m + k, src, r2.at[k, m], (lines[m], c)))
            out.append(link(base + per - 1, s1.at[hi], r2.at[1, hi_n - 1], partner))
            return out

        def step_a(parts):
            for h in range(2):
                for k, part in enumerate(parts):
                    rows = part[:, h * H:(h + 1) * H].astype(BF16).reshape(hi_n, lo_n, R, H)
                    for l in range(lo_n):
                        gb[h, l, :, :, k * H:(k + 1) * H] = rows[:, l]
            start(across())

        def step_b():
            arrived(across())
            out = plane()
            for m in range(lo_n - 1):
                at = lax.rem(lo + m + 1, lo_n)
                s0[m] = (gb[core, at].astype(F32) + r0[at].astype(F32)).astype(BF16)
                out[m].start()

        def step_c():
            arrived(plane())
            own = gb[core, lo].astype(F32) + r0[lo].astype(F32)
            for m in range(lo_n - 1):
                own = own + r1[m].astype(F32)
            s1[...] = own.astype(BF16)
            start(line())

        def step_d(put):
            arrived(line())
            mine = s1[hi].astype(F32)
            theirs = r2[1, hi_n - 1].astype(F32)
            for m in range(hi_n - 1):
                mine = mine + r2[0, m].astype(F32)
                theirs = theirs + r2[1, m].astype(F32)
            a = jnp.where(core == 0, mine, theirs) * scale
            b = jnp.where(core == 0, theirs, mine) * scale
            for k in range(a.shape[-1] // H):
                put(k, jnp.concatenate([a[:, k * H:(k + 1) * H], b[:, k * H:(k + 1) * H]], axis=-1))

        return step_a, step_b, step_c, step_d, lambda: across() + plane() + line()

    second_sum = reducer(0, big)
    first_sum = reducer(1, tap)
    pbase = 2 * per

    def pairs_p():
        return [link(pbase, q0.at[0], p0, partner)]

    def plane_p():
        return [link(pbase + 1 + m, q0.at[1], p1.at[lo], (planes[m], core)) for m in range(lo_n - 1)]

    def line_p():
        return [link(pbase + lo_n + m, q0.at[2], p2.at[hi], (lines[m], core)) for m in range(hi_n - 1)]

    def patch_a():
        q0[0] = jnp.sum(gpa[...], axis=1)
        start(pairs_p())

    def patch_b():
        arrived(pairs_p())
        q0[1] = q0[0] + p0[...]
        p1[lo] = q0[0] + p0[...]
        start(plane_p())

    def patch_c():
        arrived(plane_p())
        total = jnp.sum(p1[...], axis=0)
        q0[2] = total
        p2[hi] = total
        start(line_p())

    def patch_d():
        arrived(line_p())
        op_ref[...] = jnp.sum(p2[...], axis=0) * scale

    def mix(i, hs):
        s = order1[i]
        for c in loads[i]:
            c.wait()
        h = dot(stacked(xe, [s, s + D1, s + 2 * D1], b1), w1[...].reshape(3 * C, C))
        for t in range(2):
            hs[t, :b1 * px] = h[:, t * H:(t + 1) * H]

    def activate(i, hs):
        s = order1[i]
        g = divisor(b1, 8)
        for r in range(0, b1, g):
            for t in range(2):
                cols = slice(t * H, (t + 1) * H)
                z = None
                for j in range(4):
                    v = hs[t, pl.ds(r * px + j, g * Q, stride=4), :].astype(BF16)
                    u, sl = gelu_terms(v)
                    u_s[j, s + r:s + r + g, :, cols] = u.astype(u_s.dtype).reshape(g, Q, H)
                    s_s[j, s + r:s + r + g, :, cols] = sl.astype(s_s.dtype).reshape(g, Q, H)
                    term = (u * pwb[j:j + 1, cols]).astype(F32)
                    z = term if z is None else z + term
                z1e[s + r:s + r + g, :, cols] = z.reshape(g, Q, H).astype(BF16)

    n2 = L + 2 * HC
    b2, starts2 = blocks(n2, min(3, n2))
    order2 = sum(inner_first(starts2, b2, n2, HC), [])

    def mix2(i, h2):
        s = order2[i]
        h2[...] = dot(stacked(z1e, [s, s + D2, s + 2 * D2], b2), w2[...].reshape(3 * C, C))

    def activate2(i, h2):
        s = order2[i]
        g = divisor(b2, 8)
        for r in range(0, b2, g):
            sl = gelu_terms(h2[r * Q:(r + g) * Q, :])[1]
            d = ce[s + r:s + r + g].reshape(g * Q, C).astype(F32) * sl
            dh2e[s + r:s + r + g] = d.astype(BF16).reshape(g, Q, C)

    n3 = L + 2
    b3, order3 = blocks(n3, 4)

    def mix3(i, dz):
        s = order3[i] + HC - 1
        dz[...] = dot(stacked(dh2e, [s + D2, s, s - D2], b3), w2t[...])

    def delta(i, dz, hs):
        s = order3[i]
        done = 0 if i == 0 else order3[i - 1] + b3
        g = divisor(b3, 8)
        for r in range(0, b3, g):
            own = [b for b in range(s + r, s + r + g) if 1 <= b <= L and b >= done]
            for t in range(2):
                cols = slice(t * H, (t + 1) * H)
                d = dz[r * Q:(r + g) * Q, cols].astype(BF16)
                for j in range(4):
                    where = slice(s + r + HZ - 1, s + r + g + HZ - 1)
                    u = u_s[j, where, :, cols].reshape(g * Q, H)
                    sl = s_s[j, where, :, cols].reshape(g * Q, H)
                    hs[t, pl.ds(r * px + j, g * Q, stride=4), :] = (
                        d * pwb[j:j + 1, cols] * sl).astype(F32)
                    if own:
                        a, b = (own[0] - s - r) * Q, (own[-1] + 1 - s - r) * Q
                        m = (d[a:b] * u[a:b]).reshape(len(own), Q, H)
                        part = m[0]
                        for k in range(1, len(own)):
                            part = part + m[k]
                        gpa[j, :, cols] += part.astype(F32)
            for t in range(2):
                cols = slice(t * H, (t + 1) * H)
                dh1e[s + r:s + r + g, :, cols] = (
                    hs[t, r * px:(r + g) * px].astype(BF16).reshape(g, px, H))

    share = L // 4
    bt = max(b for b in range(1, 17) if share % b == 0 and b * px % 128 == 0)

    def turn(upto):
        while turned[0] < L // bt and (turned[0] + 1) * bt + 1 <= upto:
            i = turned[0]
            dt[:, i * bt * px:(i + 1) * bt * px] = dh1e[1 + i * bt:1 + (i + 1) * bt].reshape(bt * px, C).T
            turned[0] += 1

    turned = [0]

    def first_gradient(c):
        x = stacked(xe, [HX + c * share + k * D1 for k in (-1, 0, 1)], share)
        g = dot(dt[:, c * share * px:(c + 1) * share * px], x)
        if c == 0:
            acc1[...] = g
        elif c < 3:
            acc1[...] += g
        else:
            first_sum[0]([acc1[:, k * C:(k + 1) * C] + g[:, k * C:(k + 1) * C] for k in range(3)])

    def input_gradient_of(b, n):
        g = dot(stacked(dh1e, [b + 1 + D1, b + 1, b + 1 - D1], n), w1t[...])
        dx_ref[pl.ds(b, n)] = g.astype(BF16).reshape(n, px, C)

    first.wait()
    steps = len(order1)
    hs = [hs_a, hs_b]
    for i in range(steps + 1):
        if i < steps:
            if i == inner1:
                for c in halos():
                    c.wait()
            mix(i, hs[i % 2])
        if i == 0:
            pl.semaphore_wait(barrier, len(targets))
            for c in halos():
                c.start()
        if i == 2:
            for c in second:
                c.wait()
            turn_weights(w1, w2, w1t, w2t)
        if i:
            activate(i - 1, hs[(i - 1) % 2])

    @pl.when(core == 0)
    def _():
        z1e[pl.ds(0, HZ)] = jnp.zeros((HZ, Q, C), BF16)

    @pl.when(core == 1)
    def _():
        z1e[pl.ds(HZ + L, HZ)] = jnp.zeros((HZ, Q, C), BF16)

    h2 = [h2_a, h2_b]
    for i in range(len(order2) + 1):
        if i < len(order2):
            mix2(i, h2[i % 2])
        if i:
            activate2(i - 1, h2[(i - 1) % 2])

    dz = [dz_a, dz_b]
    mix3(0, dz[0])
    d2 = dh2e[pl.ds(HC, L)].reshape(L * Q, C)
    acc2 = dot_rows(d2, stacked(z1e, [HZ - D2, HZ, HZ + D2], L))
    second_sum[0]([acc2[:, k * C:(k + 1) * C] for k in range(3)])
    count = len(order3)
    for i in range(count):
        delta(i, dz[i % 2], hs[i % 2])
        if i + 1 < count:
            mix3(i + 1, dz[(i + 1) % 2])
            turn(order3[i] + b3)
            first_gradient(i)
        if i == 1:
            second_sum[1]()

    patch_a()

    @pl.when(core == 0)
    def _():
        dh1e[0] = jnp.zeros((px, C), BF16)

    @pl.when(core == 1)
    def _():
        dh1e[L + 1] = jnp.zeros((px, C), BF16)

    turn(n3)
    first_gradient(3)
    patch_b()
    after = [[], [first_sum[1]], [second_sum[2], patch_c], []]

    def put(q):
        def row(k, value):
            o_ref[q, k] = value
        return row

    for i in range(4):
        input_gradient_of(i * share, share)
        for hook in after[i]:
            hook()
    first_sum[2]()
    patch_d()
    second_sum[3](put(1))
    for c in second_sum[4]() + pairs_p() + plane_p() + line_p() + first_sum[4]():
        c.wait_send()
    first_sum[3](put(0))


def step_pass(scale, ndp, x, cot, w1, w2, pw):
    L, px, C = x.shape
    Q = px // 4
    H = C // 2
    R = C // ndp
    lo_n = divisor(ndp, math.isqrt(ndp))
    hi_n = ndp // lo_n
    n = 2 * (lo_n + 2 * (hi_n - 1) + 1) + lo_n + hi_n - 1
    hbm = pl.BlockSpec(memory_space=pltpu.HBM)
    vm = pl.BlockSpec(memory_space=pltpu.VMEM)
    _, b1, _, _, pieces = first_plan(L)
    b2 = blocks(L + 2 * HC, 3)[0]
    b3 = blocks(L + 2, 4)[0]
    wide = max(b1, b3)

    def sums(lead, w):
        return [
            pltpu.VMEM(lead + (2, lo_n, hi_n, R, w), BF16),
            pltpu.VMEM(lead + (lo_n, hi_n, R, w), BF16),
            pltpu.VMEM(lead + (lo_n - 1, hi_n, R, w), BF16),
            pltpu.VMEM(lead + (lo_n - 1, hi_n, R, w), BF16),
            pltpu.VMEM(lead + (hi_n, R, w), BF16),
            pltpu.VMEM(lead + (2, hi_n, R, w), BF16),
        ]

    limit = 67043328 - (L * px * C * 2 + (1 << 18))
    scratch = [
        pltpu.VMEM((L + 2 * HX, px, C), BF16),
        pltpu.VMEM((L + 2 * HC, Q, C), BF16),
        pltpu.VMEM((L + 2 * HZ, Q, C), BF16),
        pltpu.VMEM((L + 2 * HC, Q, C), BF16),
        pltpu.VMEM((L + 2, px, C), BF16),
        pltpu.VMEM((C, L * px), BF16),
        pltpu.VMEM((4, L + 2 * HZ, Q, C), BF16),
        pltpu.VMEM((4, L + 2 * HZ, Q, C), BF16),
        pltpu.VMEM((2, wide * px, H), F32),
        pltpu.VMEM((2, wide * px, H), F32),
        pltpu.VMEM((b2 * Q, C), F32),
        pltpu.VMEM((b2 * Q, C), F32),
        pltpu.VMEM((b3 * Q, C), F32),
        pltpu.VMEM((b3 * Q, C), F32),
        pltpu.VMEM((3, C, C), BF16),
        pltpu.VMEM((3, C, C), BF16),
        pltpu.VMEM((3 * C, C), BF16),
        pltpu.VMEM((3 * C, C), BF16),
        pltpu.VMEM((4, Q, C), F32),
        pltpu.SemaphoreType.DMA((sum(len(p) for p in pieces),)),
        pltpu.SemaphoreType.DMA((3,)),
        sums((), 3 * H),
        sums((), 3 * H),
        pltpu.VMEM((C, 3 * C), F32),
        pltpu.VMEM((4, C), F32),
        pltpu.VMEM((lo_n, 4, C), F32),
        pltpu.VMEM((hi_n, 4, C), F32),
        pltpu.VMEM((3, 4, C), F32),
        pltpu.SemaphoreType.DMA((2,)),
        pltpu.SemaphoreType.DMA((2,)),
        pltpu.SemaphoreType.DMA((n,)),
        pltpu.SemaphoreType.DMA((n,)),
    ]
    used = sum(math.prod(r.shape) * jnp.dtype(r.dtype).itemsize
               for r in jax.tree.leaves(scratch) if r.memory_space == pltpu.VMEM)
    spare = max((limit - used - (1 << 20)) // (8 * 128 * 4), 1) * 128
    return pl.pallas_call(
        functools.partial(step_kernel, scale, lo_n, hi_n),
        out_shape=(
            pltpu.VMEM((L, px, C), BF16),
            pltpu.VMEM((2, 3, R, C), F32),
            pltpu.VMEM((4, C), F32),
        ),
        in_specs=[hbm] * 4 + [vm],
        out_specs=[vm, vm, vm],
        scratch_shapes=scratch + [pltpu.VMEM((8, spare), F32)],
        compiler_params=pltpu.CompilerParams(
            collective_id=0, has_side_effects=True, vmem_limit_bytes=limit
        ),
        name="step_pass",
    )(x, cot, w1, w2, pw)


def hand_over_kernel(n, dx_ref, o_ref, p_ref, dx_out, o1_out, o2_out, p_out, sem):
    step = dx_ref.shape[0] // n
    out = [pltpu.make_async_copy(dx_ref.at[pl.ds(i * step, step)], dx_out.at[pl.ds(i * step, step)],
                                 sem.at[i]) for i in range(n)]
    for c in out:
        c.start()
    o1_out[...] = o_ref[0]
    o2_out[...] = o_ref[1]
    p_out[...] = p_ref[...]
    for c in out:
        c.wait()


def hand_over(dx, o, p):
    n = divisor(dx.shape[0], 4)
    vm = pl.BlockSpec(memory_space=pltpu.VMEM)
    one = jax.ShapeDtypeStruct(o.shape[1:], F32)
    dx, o1, o2, p = pl.pallas_call(
        functools.partial(hand_over_kernel, n),
        out_shape=(jax.ShapeDtypeStruct(dx.shape, dx.dtype), one, one,
                   jax.ShapeDtypeStruct(p.shape, F32)),
        in_specs=[vm, vm, vm],
        out_specs=[pl.BlockSpec(memory_space=pltpu.HBM), vm, vm, vm],
        scratch_shapes=[pltpu.SemaphoreType.DMA((n,))],
        compiler_params=pltpu.CompilerParams(vmem_limit_bytes=16 * 1024 * 1024),
        name="hand_over",
    )(dx, o, p)
    return dx, jnp.transpose(o1, (1, 0, 2)), jnp.transpose(o2, (1, 0, 2)), p


def shards(ndp, nb, x, w1, w2, pw, cot):
    L, px, C = x.shape
    Q = px // 4
    scale = 1.0 / math.sqrt(L * nb * px * ndp)
    if nb == 2 and ndp >= 4 and (C // ndp) % 16 == 0 and C % 256 == 0 and L >= 48 and L % 8 == 0 and px % 16 == 0:
        return hand_over(*step_pass(scale, ndp, x, cot, w1, w2, pw))
    up = [(i, i + 1) for i in range(nb - 1)]
    down = [(j, i) for i, j in up]

    def edges(x_part, c_part, pairs):
        both = jnp.concatenate([x_part.reshape(HX * px, C), c_part.reshape(HC * Q, C)], axis=0)
        both = lax.ppermute(both, "band", pairs)
        return both[:HX * px].reshape(HX, px, C), both[HX * px:].reshape(HC, Q, C)

    xlo, clo = edges(x[L - HX:], cot[L - HC:], up)
    xhi, chi = edges(x[:HX], cot[:HC], down)
    dx, g, gp = local_pass(nb, x, xlo, xhi, cot, clo, chi, w1, w2, pw)
    kept = lax.psum_scatter(g.astype(F32), "dp", scatter_dimension=1, tiled=True)
    kept = (lax.psum(kept, "band") * scale).reshape(2, C // ndp, 3, C)
    o1, o2 = kept[0], kept[1]
    op = lax.psum(gp, ("dp", "band")) * scale
    return dx, o1, o2, op


def solution(mesh):
    placed = (P("band", "dp", None), P(), P(), P(), P("band", "dp", None))
    return jax.shard_map(
        functools.partial(shards, mesh.shape["dp"], mesh.shape["band"]),
        mesh=mesh,
        in_specs=placed,
        out_specs=(P("band", "dp", None), P("dp", None, None), P("dp", None, None), P()),
        check_vma=False,
    )
```

```python
import functools
import math

import jax
import jax.numpy as jnp
from jax import lax
from jax.experimental import pallas as pl
from jax.experimental.pallas import tpu as pltpu
from jax.sharding import PartitionSpec as P

D1 = 1
D2 = 2
HZ = 1 + 2 * D2
HX = HZ + D1
HC = 1 + D2
MESH = pl.DeviceIdType.MESH
F32 = jnp.float32
BF16 = jnp.bfloat16
G0 = math.sqrt(2.0 / math.pi)
G1 = 0.044715 * G0


def divisor(n, most):
    return max(i for i in range(1, min(n, most) + 1) if n % i == 0)


def gelu_terms(v):
    sq = v * v
    p = 0.5 + 0.5 * jnp.tanh(v * (G0 + G1 * sq))
    u = v * p
    s = p + u * (1.0 - p) * (2.0 * G0 + (6.0 * G1) * sq)
    return u, s


def dot(a, b):
    return jnp.dot(a, b, preferred_element_type=F32)


def dot_rows(a, b):
    return lax.dot_general(a, b, (((0,), (0,)), ((), ())), preferred_element_type=F32)


def stacked(ref, starts, n):
    c = ref.shape[-1]
    return jnp.concatenate([ref[pl.ds(s, n)].reshape(-1, c) for s in starts], axis=-1)


def copy_in(pairs, sems):
    copies = [pltpu.make_async_copy(a, b, sems.at[i]) for i, (a, b) in enumerate(pairs)]
    for c in copies:
        c.start()
    return copies


def turn_weights(w1_ref, w2_ref, w1t, w2t):
    C = w1_ref.shape[-1]
    for k in range(3):
        w1t[pl.ds(k * C, C), :] = w1_ref[k].T
        w2t[pl.ds(k * C, C), :] = w2_ref[k].T


def first_layer(me, nb, early, late, xe, w1_ref, pw, hs_a, hs_b, u_s, s_s, z1e):
    n1, Q, C = z1e.shape
    L = n1 - 2 * HZ
    H = C // 2
    b1 = min(8, n1)
    steps = (n1 + b1 - 1) // b1
    edge = min((HX + L - 2 * D1) // b1, steps - 1)

    def chunk(at):
        return jnp.minimum(lax.rem(at + 1, steps) * b1, n1 - b1)

    def mix(at, hs):
        s = chunk(at)
        h = dot(stacked(xe, [s, s + D1, s + 2 * D1], b1), w1_ref[...].reshape(3 * C, C))
        for t in range(2):
            hs[t] = h[:, t * H:(t + 1) * H]

    def activate(at, hs):
        s = chunk(at)
        for t in range(2):
            z = None
            for j in range(4):
                v = hs[t, pl.ds(j, b1 * Q, stride=4), :]
                u, sl = gelu_terms(v)
                u_s[j, pl.ds(s, b1), :, t * H:(t + 1) * H] = u.reshape(b1, Q, H)
                s_s[j, pl.ds(s, b1), :, t * H:(t + 1) * H] = sl.reshape(b1, Q, H)
                term = u * pw[j:j + 1, t * H:(t + 1) * H]
                z = term if z is None else z + term
            z1e[pl.ds(s, b1), :, t * H:(t + 1) * H] = z.reshape(b1, Q, H).astype(BF16)

    mix(0, hs_a)
    pairs = (steps - 1) // 2

    @pl.loop(0, pairs)
    def _(i):
        at = 2 * i

        @pl.when(i == 0)
        def _():
            early()

        @pl.when(i == max((edge - 2) // 2, 0))
        def _():
            late()

        mix(at + 1, hs_b)
        activate(at, hs_a)
        mix(at + 2, hs_a)
        activate(at + 1, hs_b)

    if steps % 2 == 0:
        mix(steps - 1, hs_b)
    activate(2 * pairs, hs_a)
    if steps % 2 == 0:
        activate(steps - 1, hs_b)

    @pl.when(me == 0)
    def _():
        z1e[pl.ds(0, HZ)] = jnp.zeros((HZ, Q, C), BF16)

    @pl.when(me == nb - 1)
    def _():
        z1e[pl.ds(HZ + L, HZ)] = jnp.zeros((HZ, Q, C), BF16)


def second_layer(z1e, ce, w2_ref, dh2e, acc2):
    n2, Q, C = ce.shape
    L = n2 - 2 * HC
    b2 = min(16, n2)
    bg = divisor(L, b2)
    steps, gsteps = (n2 + b2 - 1) // b2, L // bg
    acc2[...] = jnp.zeros_like(acc2)

    def delta(i):
        s = jnp.minimum(i * b2, n2 - b2)
        h = dot(stacked(z1e, [s, s + D2, s + 2 * D2], b2), w2_ref[...].reshape(3 * C, C))
        sl = gelu_terms(h)[1]
        d = ce[pl.ds(s, b2)].reshape(b2 * Q, C).astype(F32) * sl
        dh2e[pl.ds(s, b2)] = d.astype(BF16).reshape(b2, Q, C)

    def weight_gradient(i):
        b = i * bg
        d = dh2e[pl.ds(b + HC, bg)].reshape(bg * Q, C)
        acc2[...] += dot_rows(d, stacked(z1e, [b + HZ - D2, b + HZ, b + HZ + D2], bg))

    lead = min(2, steps)
    both = min(steps, gsteps + lead)
    pl.loop(0, lead)(delta)

    @pl.loop(lead, both)
    def _(i):
        weight_gradient(i - lead)
        delta(i)

    pl.loop(both, steps)(delta)
    pl.loop(both - lead, gsteps)(weight_gradient)


def first_delta(me, nb, dh2e, w2t, pw, u_s, s_s, hs, gpa, dh1e, xe, acc1):
    n3, px, C = dh1e.shape
    L = n3 - 2
    Q = px // 4
    H = C // 2
    gpa[...] = jnp.zeros_like(gpa)
    acc1[...] = jnp.zeros_like(acc1)
    b3 = min(8, n3)
    bx = divisor(L, b3)
    steps, gsteps = (n3 + b3 - 1) // b3, L // bx

    def delta(i):
        s = jnp.minimum(i * b3, n3 - b3)
        o = HC - 1
        dz = dot(stacked(dh2e, [s + o + D2, s + o, s + o - D2], b3), w2t[...])
        band = s + lax.broadcasted_iota(jnp.int32, (b3, Q, 1), 0).reshape(b3 * Q, 1)
        own = (band >= jnp.maximum(1, i * b3)) & (band <= L)
        dzo = jnp.where(own, dz, 0.0)
        for t in range(2):
            cols = slice(t * H, (t + 1) * H)
            for j in range(4):
                u = u_s[j, pl.ds(s + HZ - 1, b3), :, cols].reshape(b3 * Q, H)
                sl = s_s[j, pl.ds(s + HZ - 1, b3), :, cols].reshape(b3 * Q, H)
                hs[t, pl.ds(j, b3 * Q, stride=4), :] = dz[:, cols] * pw[j:j + 1, cols] * sl
                gpa[j, :, cols] += jnp.sum((dzo[:, cols] * u).reshape(-1, 8, H), axis=0)
        for t in range(2):
            cols = slice(t * H, (t + 1) * H)
            dh1e[pl.ds(s, b3), :, cols] = hs[t].astype(BF16).reshape(b3, px, H)

    def weight_gradient(i):
        b = i * bx
        d = dh1e[pl.ds(b + 1, bx)].reshape(bx * px, C)
        acc1[...] += dot_rows(d, stacked(xe, [b + HX - D1, b + HX, b + HX + D1], bx))

    lead = min(2, steps)
    both = min(steps, gsteps + lead)
    pl.loop(0, lead)(delta)

    @pl.loop(lead, both)
    def _(i):
        weight_gradient(i - lead)
        delta(i)

    pl.loop(both, steps)(delta)

    @pl.when(me == 0)
    def _():
        dh1e[0] = jnp.zeros((px, C), BF16)

    @pl.when(me == nb - 1)
    def _():
        dh1e[L + 1] = jnp.zeros((px, C), BF16)

    pl.loop(both - lead, gsteps)(weight_gradient)


def input_gradient(dh1e, w1t, dx_ref, hooks, finish):
    L, px, C = dx_ref.shape
    bx = divisor(L, 8)
    steps = L // bx

    @pl.loop(0, steps)
    def _(i):
        for at, hook in hooks:
            pl.when(i == min(at, steps - 1))(hook)
        b = i * bx
        g = dot(stacked(dh1e, [b + 1 + D1, b + 1, b + 1 - D1], bx), w1t[...])
        dx_ref[pl.ds(b, bx)] = g.astype(BF16).reshape(bx, px, C)
        finish(pl.ds(b, bx))


def local_kernel(
    nb,
    x_hbm, xlo_hbm, xhi_hbm, cot_hbm, clo_hbm, chi_hbm, w1_ref, w2_ref, pw_ref,
    dx_ref, g_ref, gp_ref,
    xe, ce, z1e, dh2e, dh1e, u_s, s_s, hs, hs_b, w1t, w2t, acc1, acc2, gpa, sems,
):
    L, px, C = x_hbm.shape
    me = lax.axis_index("band")
    copies = copy_in([
        (xlo_hbm, xe.at[pl.ds(0, HX)]),
        (x_hbm, xe.at[pl.ds(HX, L)]),
        (xhi_hbm, xe.at[pl.ds(HX + L, HX)]),
        (clo_hbm, ce.at[pl.ds(0, HC)]),
        (cot_hbm, ce.at[pl.ds(HC, L)]),
        (chi_hbm, ce.at[pl.ds(HC + L, HC)]),
    ], sems)
    turn_weights(w1_ref, w2_ref, w1t, w2t)
    for c in copies:
        c.wait()
    pw = pw_ref[...]
    nothing = lambda *_: None
    first_layer(me, nb, nothing, nothing, xe, w1_ref, pw, hs, hs_b, u_s, s_s, z1e)
    second_layer(z1e, ce, w2_ref, dh2e, acc2)
    first_delta(me, nb, dh2e, w2t, pw, u_s, s_s, hs, gpa, dh1e, xe, acc1)
    input_gradient(dh1e, w1t, dx_ref, [], nothing)
    g_ref[0] = acc1[...].astype(BF16)
    g_ref[1] = acc2[...].astype(BF16)
    gp_ref[...] = jnp.sum(gpa[...], axis=1)


def local_scratch(L, px, C):
    Q = px // 4
    return [
        pltpu.VMEM((L + 2 * HX, px, C), BF16),
        pltpu.VMEM((L + 2 * HC, Q, C), BF16),
        pltpu.VMEM((L + 2 * HZ, Q, C), BF16),
        pltpu.VMEM((L + 2 * HC, Q, C), BF16),
        pltpu.VMEM((L + 2, px, C), BF16),
        pltpu.VMEM((4, L + 2 * HZ, Q, C), F32),
        pltpu.VMEM((4, L + 2 * HZ, Q, C), F32),
        pltpu.VMEM((2, 8 * px, C // 2), F32),
        pltpu.VMEM((2, 8 * px, C // 2), F32),
        pltpu.VMEM((3 * C, C), BF16),
        pltpu.VMEM((3 * C, C), BF16),
        pltpu.VMEM((C, 3 * C), F32),
        pltpu.VMEM((C, 3 * C), F32),
        pltpu.VMEM((4, 8, C), F32),
        pltpu.SemaphoreType.DMA((6,)),
    ]


def local_pass(nb, x, xlo, xhi, cot, clo, chi, w1, w2, pw):
    L, px, C = x.shape
    Q = px // 4
    any_spec = pl.BlockSpec(memory_space=pl.ANY)
    vm = pl.BlockSpec(memory_space=pltpu.VMEM)
    return pl.pallas_call(
        functools.partial(local_kernel, nb),
        out_shape=(
            jax.ShapeDtypeStruct((L, px, C), BF16),
            jax.ShapeDtypeStruct((2, C, 3 * C), BF16),
            jax.ShapeDtypeStruct((4, C), F32),
        ),
        in_specs=[any_spec] * 6 + [vm] * 3,
        out_specs=[vm] * 3,
        scratch_shapes=local_scratch(L, px, C),
        compiler_params=pltpu.CompilerParams(vmem_limit_bytes=60 * 1024 * 1024),
        name="local_pass",
    )(x, xlo, xhi, cot, clo, chi, w1, w2, pw)


def groups(n, most):
    return [(r, min(most, n - r)) for r in range(0, n, most)]


def blocks(n, count):
    size = -(-n // count)
    return size, [min(i * size, n - size) for i in range(count)]


def inner_first(starts, size, n, rim):
    inner = [s for s in starts if s >= rim and s + size <= n - rim]
    outer = [s for s in starts if s not in inner]
    return inner, sorted(outer, reverse=True)


def fresh(starts, size, taps, low, high):
    seen, pieces = set(), []
    for s in starts:
        rows = [r for r in range(max(s, low), min(s + size + taps, high)) if r not in seen]
        seen.update(rows)
        runs = []
        for r in rows:
            if runs and runs[-1][0] + runs[-1][1] == r:
                runs[-1][1] += 1
            else:
                runs.append([r, 1])
        pieces.append([tuple(run) for run in runs])
    rest = [r for r in range(low, high) if r not in seen]
    assert not rest
    return pieces


def first_plan(L):
    n1 = L + 2 * HZ
    size, starts = blocks(n1, min(6, n1))
    inner, outer = inner_first(starts, size, n1, HZ)
    order = inner + outer
    return n1, size, order, len(inner), fresh(order, size, 2 * D1, HX, HX + L)


def step_kernel(
    scale, lo_n, hi_n,
    x_hbm, cot_hbm, w1_hbm, w2_hbm, pw_ref,
    dx_ref, o_ref, op_ref,
    xe, ce, z1e, dh2e, dh1e, dt, u_s, s_s, hs_a, hs_b, h2_a, h2_b, dz_a, dz_b,
    w1, w2, w1t, w2t, gpa, xsem, sems,
    big, tap, acc1, p0, p1, p2, q0, hsend, hrecv, ssem, rsem, spare,
):
    L, px, C = x_hbm.shape
    Q = px // 4
    H = C // 2
    R = C // (lo_n * hi_n)
    dp = lax.axis_index("dp")
    core = lax.axis_index("band")
    other = 1 - core
    lo, hi = lax.rem(dp, lo_n), dp // lo_n
    planes = [hi * lo_n + lax.rem(lo + m, lo_n) for m in range(1, lo_n)]
    lines = [lax.rem(hi + m, hi_n) * lo_n + lo for m in range(1, hi_n)]
    partner = (dp, other)

    barrier = pltpu.get_barrier_semaphore()
    targets = [partner] + [(d, core) for d in planes] + [(d, c) for d in lines for c in (core, other)]
    for t in targets:
        pl.semaphore_signal(barrier, inc=1, device_id=t, device_id_type=MESH)

    n1, b1, order1, inner1, pieces = first_plan(L)
    first = pltpu.make_async_copy(w1_hbm, w1, sems.at[0])
    first.start()
    loads, at = [], 0
    for runs in pieces:
        mine = []
        for r, n in runs:
            c = pltpu.make_async_copy(x_hbm.at[pl.ds(r - HX, n)], xe.at[pl.ds(r, n)], xsem.at[at])
            c.start()
            mine.append(c)
            at += 1
        loads.append(mine)
    second = [pltpu.make_async_copy(w2_hbm, w2, sems.at[1]),
              pltpu.make_async_copy(cot_hbm, ce.at[pl.ds(HC, L)], sems.at[2])]
    for c in second:
        c.start()
    xpad = jnp.where(core == 0, 0, HX + L)
    cpad = jnp.where(core == 0, 0, HC + L)
    xe[pl.ds(xpad, HX)] = jnp.zeros((HX, px, C), BF16)
    ce[pl.ds(cpad, HC)] = jnp.zeros((HC, Q, C), BF16)
    gpa[...] = jnp.zeros_like(gpa)
    pw = pw_ref[...]
    pwb = pw.astype(BF16)

    def halos():
        return [
            pltpu.make_async_remote_copy(
                src_ref=src.at[pl.ds(jnp.where(core == 0, L - w, 0), w)],
                dst_ref=dst.at[pl.ds(jnp.where(core == 0, 0, w + L), w)],
                send_sem=hsend.at[i], recv_sem=hrecv.at[i],
                device_id=partner, device_id_type=MESH,
            )
            for i, (src, dst, w) in enumerate([(x_hbm, xe, HX), (cot_hbm, ce, HC)])
        ]

    def link(i, src, dst, target):
        return pltpu.make_async_remote_copy(
            src_ref=src, dst_ref=dst, send_sem=ssem.at[i], recv_sem=rsem.at[i],
            device_id=target, device_id_type=MESH,
        )

    per = 1 + (lo_n - 1) + 2 * (hi_n - 1) + 1

    def start(cs):
        for c in cs:
            c.start()

    def arrived(cs):
        for c in cs:
            c.wait_recv()

    def reducer(slot, refs):
        gb, r0, s0, r1, s1, r2 = refs
        base = slot * per

        def across():
            return [link(base, gb.at[other], r0, partner)]

        def plane():
            return [link(base + 1 + m, s0.at[m], r1.at[m], (planes[m], core))
                    for m in range(lo_n - 1)]

        def line():
            out = []
            for m in sorted(range(hi_n - 1), key=lambda m: abs(m + 1 - hi_n / 2)):
                src = s1.at[lax.rem(hi + m + 1, hi_n)]
                for k, c in enumerate((core, other)):
                    out.append(link(base + lo_n + 2 * m + k, src, r2.at[k, m], (lines[m], c)))
            out.append(link(base + per - 1, s1.at[hi], r2.at[1, hi_n - 1], partner))
            return out

        def step_a(parts):
            for h in range(2):
                for k, part in enumerate(parts):
                    rows = part[:, h * H:(h + 1) * H].astype(BF16).reshape(hi_n, lo_n, R, H)
                    for l in range(lo_n):
                        gb[h, l, :, :, k * H:(k + 1) * H] = rows[:, l]
            start(across())

        def step_b():
            arrived(across())
            out = plane()
            for m in range(lo_n - 1):
                at = lax.rem(lo + m + 1, lo_n)
                s0[m] = (gb[core, at].astype(F32) + r0[at].astype(F32)).astype(BF16)
                out[m].start()

        def step_c():
            arrived(plane())
            own = gb[core, lo].astype(F32) + r0[lo].astype(F32)
            for m in range(lo_n - 1):
                own = own + r1[m].astype(F32)
            s1[...] = own.astype(BF16)
            start(line())

        def step_d(put):
            arrived(line())
            mine = s1[hi].astype(F32)
            theirs = r2[1, hi_n - 1].astype(F32)
            for m in range(hi_n - 1):
                mine = mine + r2[0, m].astype(F32)
                theirs = theirs + r2[1, m].astype(F32)
            a = jnp.where(core == 0, mine, theirs) * scale
            b = jnp.where(core == 0, theirs, mine) * scale
            for k in range(a.shape[-1] // H):
                put(k, jnp.concatenate([a[:, k * H:(k + 1) * H], b[:, k * H:(k + 1) * H]], axis=-1))

        return step_a, step_b, step_c, step_d, lambda: across() + plane() + line()

    second_sum = reducer(0, big)
    first_sum = reducer(1, tap)
    pbase = 2 * per

    def pairs_p():
        return [link(pbase, q0.at[0], p0, partner)]

    def plane_p():
        return [link(pbase + 1 + m, q0.at[1], p1.at[lo], (planes[m], core)) for m in range(lo_n - 1)]

    def line_p():
        return [link(pbase + lo_n + m, q0.at[2], p2.at[hi], (lines[m], core)) for m in range(hi_n - 1)]

    def patch_a():
        q0[0] = jnp.sum(gpa[...], axis=1)
        start(pairs_p())

    def patch_b():
        arrived(pairs_p())
        q0[1] = q0[0] + p0[...]
        p1[lo] = q0[0] + p0[...]
        start(plane_p())

    def patch_c():
        arrived(plane_p())
        total = jnp.sum(p1[...], axis=0)
        q0[2] = total
        p2[hi] = total
        start(line_p())

    def patch_d():
        arrived(line_p())
        op_ref[...] = jnp.sum(p2[...], axis=0) * scale

    def mix(i, hs):
        s = order1[i]
        for c in loads[i]:
            c.wait()
        h = dot(stacked(xe, [s, s + D1, s + 2 * D1], b1), w1[...].reshape(3 * C, C))
        for t in range(2):
            hs[t, :b1 * px] = h[:, t * H:(t + 1) * H]

    def activate(i, hs):
        s = order1[i]
        for r, g in groups(b1, 8):
            for t in range(2):
                cols = slice(t * H, (t + 1) * H)
                z = None
                for j in range(4):
                    v = hs[t, pl.ds(r * px + j, g * Q, stride=4), :].astype(BF16)
                    u, sl = gelu_terms(v)
                    u_s[j, s + r:s + r + g, t] = u.astype(u_s.dtype).reshape(g, Q, H)
                    s_s[j, s + r:s + r + g, t] = sl.astype(s_s.dtype).reshape(g, Q, H)
                    term = (u * pwb[j:j + 1, cols]).astype(F32)
                    z = term if z is None else z + term
                z1e[s + r:s + r + g, :, cols] = z.reshape(g, Q, H).astype(BF16)

    n2 = L + 2 * HC
    b2, starts2 = blocks(n2, min(3, n2))
    order2 = sum(inner_first(starts2, b2, n2, HC), [])

    def mix2(i, h2):
        s = order2[i]
        h2[...] = dot(stacked(z1e, [s, s + D2, s + 2 * D2], b2), w2[...].reshape(3 * C, C))

    def activate2(i, h2):
        s = order2[i]
        for r, g in groups(b2, 8):
            sl = gelu_terms(h2[r * Q:(r + g) * Q, :])[1]
            d = ce[s + r:s + r + g].reshape(g * Q, C).astype(F32) * sl
            dh2e[s + r:s + r + g] = d.astype(BF16).reshape(g, Q, C)

    n3 = L + 2
    b3, order3 = blocks(n3, 4)

    def mix3(i, dz):
        s = order3[i] + HC - 1
        dz[...] = dot(stacked(dh2e, [s + D2, s, s - D2], b3), w2t[...])

    def delta(i, dz, hs):
        s = order3[i]
        done = 0 if i == 0 else order3[i - 1] + b3
        for r, g in groups(b3, 8):
            own = [b for b in range(s + r, s + r + g) if 1 <= b <= L and b >= done]
            for t in range(2):
                cols = slice(t * H, (t + 1) * H)
                d = dz[r * Q:(r + g) * Q, cols].astype(BF16)
                for j in range(4):
                    where = slice(s + r + HZ - 1, s + r + g + HZ - 1)
                    u = u_s[j, where, t].reshape(g * Q, H)
                    sl = s_s[j, where, t].reshape(g * Q, H)
                    hs[t, pl.ds(r * px + j, g * Q, stride=4), :] = (
                        d * pwb[j:j + 1, cols] * sl).astype(F32)
                    if own:
                        a, b = (own[0] - s - r) * Q, (own[-1] + 1 - s - r) * Q
                        m = (d[a:b] * u[a:b]).reshape(len(own), Q, H)
                        part = m[0]
                        for k in range(1, len(own)):
                            part = part + m[k]
                        gpa[j, :, cols] += part.astype(F32)
            for t in range(2):
                dh1e[s + r:s + r + g, t] = (
                    hs[t, r * px:(r + g) * px].astype(BF16).reshape(g, px, H))

    share = L // 4
    bt = max(b for b in range(1, 17) if share % b == 0 and b * px % 128 == 0)

    def turn(upto):
        while turned[0] < L // bt and (turned[0] + 1) * bt + 1 <= upto:
            i = turned[0]
            for t in range(2):
                part = dh1e[1 + i * bt:1 + (i + 1) * bt, t].reshape(bt * px, H)
                dt[t * H:(t + 1) * H, i * bt * px:(i + 1) * bt * px] = part.T
            turned[0] += 1

    turned = [0]

    def first_gradient(c):
        x = stacked(xe, [HX + c * share + k * D1 for k in (-1, 0, 1)], share)
        g = dot(dt[:, c * share * px:(c + 1) * share * px], x)
        if c == 0:
            acc1[...] = g
        elif c < 3:
            acc1[...] += g
        else:
            first_sum[0]([acc1[:, k * C:(k + 1) * C] + g[:, k * C:(k + 1) * C] for k in range(3)])

    def input_gradient_of(b, n):
        parts = [dh1e[pl.ds(at, n), t].reshape(n * px, H)
                 for at in (b + 1 + D1, b + 1, b + 1 - D1) for t in range(2)]
        g = dot(jnp.concatenate(parts, axis=-1), w1t[...])
        dx_ref[pl.ds(b, n)] = g.astype(BF16).reshape(n, px, C)

    first.wait()
    steps = len(order1)
    hs = [hs_a, hs_b]
    h2 = [h2_a, h2_b]
    for i in range(steps):
        if i == inner1:
            for c in halos():
                c.wait()
        if i == min(2, steps - 1):
            for c in second:
                c.wait()
        mix(i, hs[i % 2])
        if i == 0:
            pl.semaphore_wait(barrier, len(targets))
            for c in halos():
                c.start()
        if i == min(2, steps - 1):
            turn_weights(w1, w2, w1t, w2t)
        if i:
            activate(i - 1, hs[(i - 1) % 2])

    reach = order2[0] + b2 + 2 * D2
    apart = order1[-1] + b1 <= order2[0] or reach <= order1[-1]
    early = apart and order2[0] >= HZ and reach <= HZ + L
    if early:
        mix2(0, h2[0])
    activate(steps - 1, hs[(steps - 1) % 2])
    z1e[pl.ds(jnp.where(core == 0, 0, HZ + L), HZ)] = jnp.zeros((HZ, Q, C), BF16)
    if not early:
        mix2(0, h2[0])
    for i in range(len(order2)):
        if i + 1 < len(order2):
            mix2(i + 1, h2[(i + 1) % 2])
        activate2(i, h2[i % 2])

    dz = [dz_a, dz_b]
    mix3(0, dz[0])
    d2 = dh2e[pl.ds(HC, L)].reshape(L * Q, C)
    acc2 = dot_rows(d2, stacked(z1e, [HZ - D2, HZ, HZ + D2], L))
    delta(0, dz[0], hs[0])
    second_sum[0]([acc2[:, k * C:(k + 1) * C] for k in range(3)])
    count = len(order3)
    for i in range(count):
        if i:
            delta(i, dz[i % 2], hs[i % 2])
        if i + 1 < count:
            mix3(i + 1, dz[(i + 1) % 2])
            turn(order3[i] + b3)
            first_gradient(i)
        if i == 1:
            second_sum[1]()

    turn(n3)
    first_gradient(3)
    patch_a()
    dh1e[jnp.where(core == 0, 0, L + 1)] = jnp.zeros((2, px, H), BF16)
    after = [[patch_b], [first_sum[1]], [second_sum[2], patch_c], []]

    def put(q):
        def row(k, value):
            o_ref[q, k] = value
        return row

    for i in range(4):
        input_gradient_of(i * share, share)
        for hook in after[i]:
            hook()
    first_sum[2]()
    patch_d()
    second_sum[3](put(1))
    for c in second_sum[4]() + pairs_p() + plane_p() + line_p() + first_sum[4]():
        c.wait_send()
    first_sum[3](put(0))


def step_pass(scale, ndp, x, cot, w1, w2, pw):
    L, px, C = x.shape
    Q = px // 4
    H = C // 2
    R = C // ndp
    lo_n = divisor(ndp, math.isqrt(ndp))
    hi_n = ndp // lo_n
    n = 2 * (lo_n + 2 * (hi_n - 1) + 1) + lo_n + hi_n - 1
    hbm = pl.BlockSpec(memory_space=pltpu.HBM)
    vm = pl.BlockSpec(memory_space=pltpu.VMEM)
    _, b1, _, _, pieces = first_plan(L)
    b2 = blocks(L + 2 * HC, 3)[0]
    b3 = blocks(L + 2, 4)[0]
    wide = max(b1, b3)

    def sums(lead, w):
        return [
            pltpu.VMEM(lead + (2, lo_n, hi_n, R, w), BF16),
            pltpu.VMEM(lead + (lo_n, hi_n, R, w), BF16),
            pltpu.VMEM(lead + (lo_n - 1, hi_n, R, w), BF16),
            pltpu.VMEM(lead + (lo_n - 1, hi_n, R, w), BF16),
            pltpu.VMEM(lead + (hi_n, R, w), BF16),
            pltpu.VMEM(lead + (2, hi_n, R, w), BF16),
        ]

    limit = 67043328 - (L * px * C * 2 + (1 << 18))
    scratch = [
        pltpu.VMEM((L + 2 * HX, px, C), BF16),
        pltpu.VMEM((L + 2 * HC, Q, C), BF16),
        pltpu.VMEM((L + 2 * HZ, Q, C), BF16),
        pltpu.VMEM((L + 2 * HC, Q, C), BF16),
        pltpu.VMEM((L + 2, 2, px, H), BF16),
        pltpu.VMEM((C, L * px), BF16),
        pltpu.VMEM((4, L + 2 * HZ, 2, Q, H), BF16),
        pltpu.VMEM((4, L + 2 * HZ, 2, Q, H), BF16),
        pltpu.VMEM((2, wide * px, H), F32),
        pltpu.VMEM((2, wide * px, H), F32),
        pltpu.VMEM((b2 * Q, C), F32),
        pltpu.VMEM((b2 * Q, C), F32),
        pltpu.VMEM((b3 * Q, C), F32),
        pltpu.VMEM((b3 * Q, C), F32),
        pltpu.VMEM((3, C, C), BF16),
        pltpu.VMEM((3, C, C), BF16),
        pltpu.VMEM((3 * C, C), BF16),
        pltpu.VMEM((3 * C, C), BF16),
        pltpu.VMEM((4, Q, C), F32),
        pltpu.SemaphoreType.DMA((sum(len(p) for p in pieces),)),
        pltpu.SemaphoreType.DMA((3,)),
        sums((), 3 * H),
        sums((), 3 * H),
        pltpu.VMEM((C, 3 * C), F32),
        pltpu.VMEM((4, C), F32),
        pltpu.VMEM((lo_n, 4, C), F32),
        pltpu.VMEM((hi_n, 4, C), F32),
        pltpu.VMEM((3, 4, C), F32),
        pltpu.SemaphoreType.DMA((2,)),
        pltpu.SemaphoreType.DMA((2,)),
        pltpu.SemaphoreType.DMA((n,)),
        pltpu.SemaphoreType.DMA((n,)),
    ]
    used = sum(math.prod(r.shape) * jnp.dtype(r.dtype).itemsize
               for r in jax.tree.leaves(scratch) if r.memory_space == pltpu.VMEM)
    spare = max((limit - used - (1 << 20)) // (8 * 128 * 4), 1) * 128
    return pl.pallas_call(
        functools.partial(step_kernel, scale, lo_n, hi_n),
        out_shape=(
            pltpu.VMEM((L, px, C), BF16),
            pltpu.VMEM((2, 3, R, C), F32),
            pltpu.VMEM((4, C), F32),
        ),
        in_specs=[hbm] * 4 + [vm],
        out_specs=[vm, vm, vm],
        scratch_shapes=scratch + [pltpu.VMEM((8, spare), F32)],
        compiler_params=pltpu.CompilerParams(
            collective_id=0, has_side_effects=True, vmem_limit_bytes=limit
        ),
        name="step_pass",
    )(x, cot, w1, w2, pw)


def hand_over_kernel(n, dx_ref, o_ref, p_ref, dx_out, o1_out, o2_out, p_out, sem):
    step = dx_ref.shape[0] // n
    out = [pltpu.make_async_copy(dx_ref.at[pl.ds(i * step, step)], dx_out.at[pl.ds(i * step, step)],
                                 sem.at[i]) for i in range(n)]
    for c in out:
        c.start()
    o1_out[...] = o_ref[0]
    o2_out[...] = o_ref[1]
    p_out[...] = p_ref[...]
    for c in out:
        c.wait()


def hand_over(dx, o, p):
    n = divisor(dx.shape[0], 4)
    vm = pl.BlockSpec(memory_space=pltpu.VMEM)
    one = jax.ShapeDtypeStruct(o.shape[1:], F32)
    dx, o1, o2, p = pl.pallas_call(
        functools.partial(hand_over_kernel, n),
        out_shape=(jax.ShapeDtypeStruct(dx.shape, dx.dtype), one, one,
                   jax.ShapeDtypeStruct(p.shape, F32)),
        in_specs=[vm, vm, vm],
        out_specs=[pl.BlockSpec(memory_space=pltpu.HBM), vm, vm, vm],
        scratch_shapes=[pltpu.SemaphoreType.DMA((n,))],
        compiler_params=pltpu.CompilerParams(vmem_limit_bytes=16 * 1024 * 1024),
        name="hand_over",
    )(dx, o, p)
    return dx, jnp.transpose(o1, (1, 0, 2)), jnp.transpose(o2, (1, 0, 2)), p


def shards(ndp, nb, x, w1, w2, pw, cot):
    L, px, C = x.shape
    Q = px // 4
    scale = 1.0 / math.sqrt(L * nb * px * ndp)
    if nb == 2 and ndp >= 4 and (C // ndp) % 16 == 0 and C % 256 == 0 and L >= 48 and L % 8 == 0 and px % 16 == 0:
        return hand_over(*step_pass(scale, ndp, x, cot, w1, w2, pw))
    up = [(i, i + 1) for i in range(nb - 1)]
    down = [(j, i) for i, j in up]

    def edges(x_part, c_part, pairs):
        both = jnp.concatenate([x_part.reshape(HX * px, C), c_part.reshape(HC * Q, C)], axis=0)
        both = lax.ppermute(both, "band", pairs)
        return both[:HX * px].reshape(HX, px, C), both[HX * px:].reshape(HC, Q, C)

    xlo, clo = edges(x[L - HX:], cot[L - HC:], up)
    xhi, chi = edges(x[:HX], cot[:HC], down)
    dx, g, gp = local_pass(nb, x, xlo, xhi, cot, clo, chi, w1, w2, pw)
    kept = lax.psum_scatter(g.astype(F32), "dp", scatter_dimension=1, tiled=True)
    kept = (lax.psum(kept, "band") * scale).reshape(2, C // ndp, 3, C)
    o1, o2 = kept[0], kept[1]
    op = lax.psum(gp, ("dp", "band")) * scale
    return dx, o1, o2, op


def solution(mesh):
    placed = (P("band", "dp", None), P(), P(), P(), P("band", "dp", None))
    return jax.shard_map(
        functools.partial(shards, mesh.shape["dp"], mesh.shape["band"]),
        mesh=mesh,
        in_specs=placed,
        out_specs=(P("band", "dp", None), P("dp", None, None), P("dp", None, None), P()),
        check_vma=False,
    )
```

```python
import functools
import math

import jax
import jax.numpy as jnp
from jax import lax
from jax.experimental import pallas as pl
from jax.experimental.pallas import tpu as pltpu
from jax.sharding import PartitionSpec as P

D1 = 1
D2 = 2
HZ = 1 + 2 * D2
HX = HZ + D1
HC = 1 + D2
MESH = pl.DeviceIdType.MESH
F32 = jnp.float32
BF16 = jnp.bfloat16
G0 = math.sqrt(2.0 / math.pi)
G1 = 0.044715 * G0


def divisor(n, most):
    return max(i for i in range(1, min(n, most) + 1) if n % i == 0)


def gelu_terms(v):
    sq = v * v
    p = 0.5 + 0.5 * jnp.tanh(v * (G0 + G1 * sq))
    u = v * p
    s = p + u * (1.0 - p) * (2.0 * G0 + (6.0 * G1) * sq)
    return u, s


def dot(a, b):
    return jnp.dot(a, b, preferred_element_type=F32)


def dot_rows(a, b):
    return lax.dot_general(a, b, (((0,), (0,)), ((), ())), preferred_element_type=F32)


def stacked(ref, starts, n):
    c = ref.shape[-1]
    return jnp.concatenate([ref[pl.ds(s, n)].reshape(-1, c) for s in starts], axis=-1)


def copy_in(pairs, sems):
    copies = [pltpu.make_async_copy(a, b, sems.at[i]) for i, (a, b) in enumerate(pairs)]
    for c in copies:
        c.start()
    return copies


def turn_weights(w1_ref, w2_ref, w1t, w2t):
    C = w1_ref.shape[-1]
    for k in range(3):
        w1t[pl.ds(k * C, C), :] = w1_ref[k].T
        w2t[pl.ds(k * C, C), :] = w2_ref[k].T


def first_layer(me, nb, early, late, xe, w1_ref, pw, hs_a, hs_b, u_s, s_s, z1e):
    n1, Q, C = z1e.shape
    L = n1 - 2 * HZ
    H = C // 2
    b1 = min(8, n1)
    steps = (n1 + b1 - 1) // b1
    edge = min((HX + L - 2 * D1) // b1, steps - 1)

    def chunk(at):
        return jnp.minimum(lax.rem(at + 1, steps) * b1, n1 - b1)

    def mix(at, hs):
        s = chunk(at)
        h = dot(stacked(xe, [s, s + D1, s + 2 * D1], b1), w1_ref[...].reshape(3 * C, C))
        for t in range(2):
            hs[t] = h[:, t * H:(t + 1) * H]

    def activate(at, hs):
        s = chunk(at)
        for t in range(2):
            z = None
            for j in range(4):
                v = hs[t, pl.ds(j, b1 * Q, stride=4), :]
                u, sl = gelu_terms(v)
                u_s[j, pl.ds(s, b1), :, t * H:(t + 1) * H] = u.reshape(b1, Q, H)
                s_s[j, pl.ds(s, b1), :, t * H:(t + 1) * H] = sl.reshape(b1, Q, H)
                term = u * pw[j:j + 1, t * H:(t + 1) * H]
                z = term if z is None else z + term
            z1e[pl.ds(s, b1), :, t * H:(t + 1) * H] = z.reshape(b1, Q, H).astype(BF16)

    mix(0, hs_a)
    pairs = (steps - 1) // 2

    @pl.loop(0, pairs)
    def _(i):
        at = 2 * i

        @pl.when(i == 0)
        def _():
            early()

        @pl.when(i == max((edge - 2) // 2, 0))
        def _():
            late()

        mix(at + 1, hs_b)
        activate(at, hs_a)
        mix(at + 2, hs_a)
        activate(at + 1, hs_b)

    if steps % 2 == 0:
        mix(steps - 1, hs_b)
    activate(2 * pairs, hs_a)
    if steps % 2 == 0:
        activate(steps - 1, hs_b)

    @pl.when(me == 0)
    def _():
        z1e[pl.ds(0, HZ)] = jnp.zeros((HZ, Q, C), BF16)

    @pl.when(me == nb - 1)
    def _():
        z1e[pl.ds(HZ + L, HZ)] = jnp.zeros((HZ, Q, C), BF16)


def second_layer(z1e, ce, w2_ref, dh2e, acc2):
    n2, Q, C = ce.shape
    L = n2 - 2 * HC
    b2 = min(16, n2)
    bg = divisor(L, b2)
    steps, gsteps = (n2 + b2 - 1) // b2, L // bg
    acc2[...] = jnp.zeros_like(acc2)

    def delta(i):
        s = jnp.minimum(i * b2, n2 - b2)
        h = dot(stacked(z1e, [s, s + D2, s + 2 * D2], b2), w2_ref[...].reshape(3 * C, C))
        sl = gelu_terms(h)[1]
        d = ce[pl.ds(s, b2)].reshape(b2 * Q, C).astype(F32) * sl
        dh2e[pl.ds(s, b2)] = d.astype(BF16).reshape(b2, Q, C)

    def weight_gradient(i):
        b = i * bg
        d = dh2e[pl.ds(b + HC, bg)].reshape(bg * Q, C)
        acc2[...] += dot_rows(d, stacked(z1e, [b + HZ - D2, b + HZ, b + HZ + D2], bg))

    lead = min(2, steps)
    both = min(steps, gsteps + lead)
    pl.loop(0, lead)(delta)

    @pl.loop(lead, both)
    def _(i):
        weight_gradient(i - lead)
        delta(i)

    pl.loop(both, steps)(delta)
    pl.loop(both - lead, gsteps)(weight_gradient)


def first_delta(me, nb, dh2e, w2t, pw, u_s, s_s, hs, gpa, dh1e, xe, acc1):
    n3, px, C = dh1e.shape
    L = n3 - 2
    Q = px // 4
    H = C // 2
    gpa[...] = jnp.zeros_like(gpa)
    acc1[...] = jnp.zeros_like(acc1)
    b3 = min(8, n3)
    bx = divisor(L, b3)
    steps, gsteps = (n3 + b3 - 1) // b3, L // bx

    def delta(i):
        s = jnp.minimum(i * b3, n3 - b3)
        o = HC - 1
        dz = dot(stacked(dh2e, [s + o + D2, s + o, s + o - D2], b3), w2t[...])
        band = s + lax.broadcasted_iota(jnp.int32, (b3, Q, 1), 0).reshape(b3 * Q, 1)
        own = (band >= jnp.maximum(1, i * b3)) & (band <= L)
        dzo = jnp.where(own, dz, 0.0)
        for t in range(2):
            cols = slice(t * H, (t + 1) * H)
            for j in range(4):
                u = u_s[j, pl.ds(s + HZ - 1, b3), :, cols].reshape(b3 * Q, H)
                sl = s_s[j, pl.ds(s + HZ - 1, b3), :, cols].reshape(b3 * Q, H)
                hs[t, pl.ds(j, b3 * Q, stride=4), :] = dz[:, cols] * pw[j:j + 1, cols] * sl
                gpa[j, :, cols] += jnp.sum((dzo[:, cols] * u).reshape(-1, 8, H), axis=0)
        for t in range(2):
            cols = slice(t * H, (t + 1) * H)
            dh1e[pl.ds(s, b3), :, cols] = hs[t].astype(BF16).reshape(b3, px, H)

    def weight_gradient(i):
        b = i * bx
        d = dh1e[pl.ds(b + 1, bx)].reshape(bx * px, C)
        acc1[...] += dot_rows(d, stacked(xe, [b + HX - D1, b + HX, b + HX + D1], bx))

    lead = min(2, steps)
    both = min(steps, gsteps + lead)
    pl.loop(0, lead)(delta)

    @pl.loop(lead, both)
    def _(i):
        weight_gradient(i - lead)
        delta(i)

    pl.loop(both, steps)(delta)

    @pl.when(me == 0)
    def _():
        dh1e[0] = jnp.zeros((px, C), BF16)

    @pl.when(me == nb - 1)
    def _():
        dh1e[L + 1] = jnp.zeros((px, C), BF16)

    pl.loop(both - lead, gsteps)(weight_gradient)


def input_gradient(dh1e, w1t, dx_ref, hooks, finish):
    L, px, C = dx_ref.shape
    bx = divisor(L, 8)
    steps = L // bx

    @pl.loop(0, steps)
    def _(i):
        for at, hook in hooks:
            pl.when(i == min(at, steps - 1))(hook)
        b = i * bx
        g = dot(stacked(dh1e, [b + 1 + D1, b + 1, b + 1 - D1], bx), w1t[...])
        dx_ref[pl.ds(b, bx)] = g.astype(BF16).reshape(bx, px, C)
        finish(pl.ds(b, bx))


def local_kernel(
    nb,
    x_hbm, xlo_hbm, xhi_hbm, cot_hbm, clo_hbm, chi_hbm, w1_ref, w2_ref, pw_ref,
    dx_ref, g_ref, gp_ref,
    xe, ce, z1e, dh2e, dh1e, u_s, s_s, hs, hs_b, w1t, w2t, acc1, acc2, gpa, sems,
):
    L, px, C = x_hbm.shape
    me = lax.axis_index("band")
    copies = copy_in([
        (xlo_hbm, xe.at[pl.ds(0, HX)]),
        (x_hbm, xe.at[pl.ds(HX, L)]),
        (xhi_hbm, xe.at[pl.ds(HX + L, HX)]),
        (clo_hbm, ce.at[pl.ds(0, HC)]),
        (cot_hbm, ce.at[pl.ds(HC, L)]),
        (chi_hbm, ce.at[pl.ds(HC + L, HC)]),
    ], sems)
    turn_weights(w1_ref, w2_ref, w1t, w2t)
    for c in copies:
        c.wait()
    pw = pw_ref[...]
    nothing = lambda *_: None
    first_layer(me, nb, nothing, nothing, xe, w1_ref, pw, hs, hs_b, u_s, s_s, z1e)
    second_layer(z1e, ce, w2_ref, dh2e, acc2)
    first_delta(me, nb, dh2e, w2t, pw, u_s, s_s, hs, gpa, dh1e, xe, acc1)
    input_gradient(dh1e, w1t, dx_ref, [], nothing)
    g_ref[0] = acc1[...].astype(BF16)
    g_ref[1] = acc2[...].astype(BF16)
    gp_ref[...] = jnp.sum(gpa[...], axis=1)


def local_scratch(L, px, C):
    Q = px // 4
    return [
        pltpu.VMEM((L + 2 * HX, px, C), BF16),
        pltpu.VMEM((L + 2 * HC, Q, C), BF16),
        pltpu.VMEM((L + 2 * HZ, Q, C), BF16),
        pltpu.VMEM((L + 2 * HC, Q, C), BF16),
        pltpu.VMEM((L + 2, px, C), BF16),
        pltpu.VMEM((4, L + 2 * HZ, Q, C), F32),
        pltpu.VMEM((4, L + 2 * HZ, Q, C), F32),
        pltpu.VMEM((2, 8 * px, C // 2), F32),
        pltpu.VMEM((2, 8 * px, C // 2), F32),
        pltpu.VMEM((3 * C, C), BF16),
        pltpu.VMEM((3 * C, C), BF16),
        pltpu.VMEM((C, 3 * C), F32),
        pltpu.VMEM((C, 3 * C), F32),
        pltpu.VMEM((4, 8, C), F32),
        pltpu.SemaphoreType.DMA((6,)),
    ]


def local_pass(nb, x, xlo, xhi, cot, clo, chi, w1, w2, pw):
    L, px, C = x.shape
    Q = px // 4
    any_spec = pl.BlockSpec(memory_space=pl.ANY)
    vm = pl.BlockSpec(memory_space=pltpu.VMEM)
    return pl.pallas_call(
        functools.partial(local_kernel, nb),
        out_shape=(
            jax.ShapeDtypeStruct((L, px, C), BF16),
            jax.ShapeDtypeStruct((2, C, 3 * C), BF16),
            jax.ShapeDtypeStruct((4, C), F32),
        ),
        in_specs=[any_spec] * 6 + [vm] * 3,
        out_specs=[vm] * 3,
        scratch_shapes=local_scratch(L, px, C),
        compiler_params=pltpu.CompilerParams(vmem_limit_bytes=60 * 1024 * 1024),
        name="local_pass",
    )(x, xlo, xhi, cot, clo, chi, w1, w2, pw)


def groups(n, most):
    return [(r, min(most, n - r)) for r in range(0, n, most)]


def blocks(n, count):
    size = -(-n // count)
    return size, [min(i * size, n - size) for i in range(count)]


def inner_first(starts, size, n, rim):
    inner = [s for s in starts if s >= rim and s + size <= n - rim]
    outer = [s for s in starts if s not in inner]
    return inner, sorted(outer, reverse=True)


def fresh(starts, size, taps, low, high):
    seen, pieces = set(), []
    for s in starts:
        rows = [r for r in range(max(s, low), min(s + size + taps, high)) if r not in seen]
        seen.update(rows)
        runs = []
        for r in rows:
            if runs and runs[-1][0] + runs[-1][1] == r:
                runs[-1][1] += 1
            else:
                runs.append([r, 1])
        pieces.append([tuple(run) for run in runs])
    rest = [r for r in range(low, high) if r not in seen]
    assert not rest
    return pieces


def first_plan(L):
    n1 = L + 2 * HZ
    size, starts = blocks(n1, min(5, n1))
    inner, outer = inner_first(starts, size, n1, HZ)
    order = inner + outer
    return n1, size, order, len(inner), fresh(order, size, 2 * D1, HX, HX + L)


def step_kernel(
    scale, lo_n, hi_n,
    x_hbm, cot_hbm, w1_hbm, w2_hbm, pw_ref,
    dx_ref, o_ref, op_ref,
    xe, ce, z1e, dh2e, dh1e, dt, u_s, s_s, hs_a, hs_b, h2_a, h2_b, dz_a, dz_b,
    w1, w2, w1t, w2t, gpa, xsem, sems,
    big, tap, acc1, p0, p1, p2, q0, hsend, hrecv, ssem, rsem, spare,
):
    L, px, C = x_hbm.shape
    Q = px // 4
    H = C // 2
    R = C // (lo_n * hi_n)
    dp = lax.axis_index("dp")
    core = lax.axis_index("band")
    other = 1 - core
    lo, hi = lax.rem(dp, lo_n), dp // lo_n
    planes = [hi * lo_n + lax.rem(lo + m, lo_n) for m in range(1, lo_n)]
    lines = [lax.rem(hi + m, hi_n) * lo_n + lo for m in range(1, hi_n)]
    partner = (dp, other)

    barrier = pltpu.get_barrier_semaphore()
    targets = [partner] + [(d, core) for d in planes] + [(d, c) for d in lines for c in (core, other)]
    for t in targets:
        pl.semaphore_signal(barrier, inc=1, device_id=t, device_id_type=MESH)

    n1, b1, order1, inner1, pieces = first_plan(L)
    first = pltpu.make_async_copy(w1_hbm, w1, sems.at[0])
    first.start()
    loads, at = [], 0
    for runs in pieces:
        mine = []
        for r, n in runs:
            c = pltpu.make_async_copy(x_hbm.at[pl.ds(r - HX, n)], xe.at[pl.ds(r, n)], xsem.at[at])
            c.start()
            mine.append(c)
            at += 1
        loads.append(mine)
    second = [pltpu.make_async_copy(w2_hbm, w2, sems.at[1]),
              pltpu.make_async_copy(cot_hbm, ce.at[pl.ds(HC, L)], sems.at[2])]
    for c in second:
        c.start()
    xpad = jnp.where(core == 0, 0, HX + L)
    cpad = jnp.where(core == 0, 0, HC + L)
    xe[pl.ds(xpad, HX)] = jnp.zeros((HX, px, C), BF16)
    ce[pl.ds(cpad, HC)] = jnp.zeros((HC, Q, C), BF16)
    gpa[...] = jnp.zeros_like(gpa)
    pw = pw_ref[...]
    pwb = pw.astype(BF16)

    def halos():
        return [
            pltpu.make_async_remote_copy(
                src_ref=src.at[pl.ds(jnp.where(core == 0, L - w, 0), w)],
                dst_ref=dst.at[pl.ds(jnp.where(core == 0, 0, w + L), w)],
                send_sem=hsend.at[i], recv_sem=hrecv.at[i],
                device_id=partner, device_id_type=MESH,
            )
            for i, (src, dst, w) in enumerate([(x_hbm, xe, HX), (cot_hbm, ce, HC)])
        ]

    def link(i, src, dst, target):
        return pltpu.make_async_remote_copy(
            src_ref=src, dst_ref=dst, send_sem=ssem.at[i], recv_sem=rsem.at[i],
            device_id=target, device_id_type=MESH,
        )

    per = 1 + (lo_n - 1) + 2 * (hi_n - 1) + 1

    def start(cs):
        for c in cs:
            c.start()

    def arrived(cs):
        for c in cs:
            c.wait_recv()

    def reducer(slot, refs):
        gb, r0, s0, r1, s1, r2 = refs
        base = slot * per

        def across():
            return [link(base, gb.at[other], r0, partner)]

        def plane():
            return [link(base + 1 + m, s0.at[m], r1.at[m], (planes[m], core))
                    for m in range(lo_n - 1)]

        def line():
            out = []
            for m in sorted(range(hi_n - 1), key=lambda m: abs(m + 1 - hi_n / 2)):
                src = s1.at[lax.rem(hi + m + 1, hi_n)]
                for k, c in enumerate((core, other)):
                    out.append(link(base + lo_n + 2 * m + k, src, r2.at[k, m], (lines[m], c)))
            out.append(link(base + per - 1, s1.at[hi], r2.at[1, hi_n - 1], partner))
            return out

        def step_a(parts):
            for h in range(2):
                for k, part in enumerate(parts):
                    rows = part[:, h * H:(h + 1) * H].astype(BF16).reshape(hi_n, lo_n, R, H)
                    for l in range(lo_n):
                        gb[h, l, :, :, k * H:(k + 1) * H] = rows[:, l]
            start(across())

        def step_b():
            arrived(across())
            out = plane()
            for m in range(lo_n - 1):
                at = lax.rem(lo + m + 1, lo_n)
                s0[m] = (gb[core, at].astype(F32) + r0[at].astype(F32)).astype(BF16)
                out[m].start()

        def step_c():
            arrived(plane())
            own = gb[core, lo].astype(F32) + r0[lo].astype(F32)
            for m in range(lo_n - 1):
                own = own + r1[m].astype(F32)
            s1[...] = own.astype(BF16)
            start(line())

        def step_d(put):
            arrived(line())
            mine = s1[hi].astype(F32)
            theirs = r2[1, hi_n - 1].astype(F32)
            for m in range(hi_n - 1):
                mine = mine + r2[0, m].astype(F32)
                theirs = theirs + r2[1, m].astype(F32)
            a = jnp.where(core == 0, mine, theirs) * scale
            b = jnp.where(core == 0, theirs, mine) * scale
            for k in range(a.shape[-1] // H):
                put(k, jnp.concatenate([a[:, k * H:(k + 1) * H], b[:, k * H:(k + 1) * H]], axis=-1))

        return step_a, step_b, step_c, step_d, lambda: across() + plane() + line()

    second_sum = reducer(0, big)
    first_sum = reducer(1, tap)
    pbase = 2 * per

    def pairs_p():
        return [link(pbase, q0.at[0], p0, partner)]

    def plane_p():
        return [link(pbase + 1 + m, q0.at[1], p1.at[lo], (planes[m], core)) for m in range(lo_n - 1)]

    def line_p():
        return [link(pbase + lo_n + m, q0.at[2], p2.at[hi], (lines[m], core)) for m in range(hi_n - 1)]

    def patch_a():
        q0[0] = jnp.sum(gpa[...], axis=1)
        start(pairs_p())

    def patch_b():
        arrived(pairs_p())
        q0[1] = q0[0] + p0[...]
        p1[lo] = q0[0] + p0[...]
        start(plane_p())

    def patch_c():
        arrived(plane_p())
        total = jnp.sum(p1[...], axis=0)
        q0[2] = total
        p2[hi] = total
        start(line_p())

    def patch_d():
        arrived(line_p())
        op_ref[...] = jnp.sum(p2[...], axis=0) * scale

    def mix(i, hs):
        s = order1[i]
        for c in loads[i]:
            c.wait()
        h = dot(stacked(xe, [s, s + D1, s + 2 * D1], b1), w1[...].reshape(3 * C, C))
        for t in range(2):
            hs[t, :b1 * px] = h[:, t * H:(t + 1) * H]

    def activate(i, hs):
        s = order1[i]
        for r, g in groups(b1, 8):
            for t in range(2):
                cols = slice(t * H, (t + 1) * H)
                z = None
                for j in range(4):
                    v = hs[t, pl.ds(r * px + j, g * Q, stride=4), :].astype(BF16)
                    u, sl = gelu_terms(v)
                    u_s[j, s + r:s + r + g, t] = u.astype(u_s.dtype).reshape(g, Q, H)
                    s_s[j, s + r:s + r + g, t] = sl.astype(s_s.dtype).reshape(g, Q, H)
                    term = (u * pwb[j:j + 1, cols]).astype(F32)
                    z = term if z is None else z + term
                z1e[s + r:s + r + g, :, cols] = z.reshape(g, Q, H).astype(BF16)

    n2 = L + 2 * HC
    b2, starts2 = blocks(n2, min(3, n2))
    order2 = sum(inner_first(starts2, b2, n2, HC), [])

    def mix2(i, h2):
        s = order2[i]
        h2[...] = dot(stacked(z1e, [s, s + D2, s + 2 * D2], b2), w2[...].reshape(3 * C, C))

    def activate2(i, h2):
        s = order2[i]
        for r, g in groups(b2, 8):
            sl = gelu_terms(h2[r * Q:(r + g) * Q, :])[1]
            d = ce[s + r:s + r + g].reshape(g * Q, C).astype(F32) * sl
            dh2e[s + r:s + r + g] = d.astype(BF16).reshape(g, Q, C)

    n3 = L + 2
    b3, order3 = blocks(n3, 4)

    def mix3(i, dz):
        s = order3[i] + HC - 1
        dz[...] = dot(stacked(dh2e, [s + D2, s, s - D2], b3), w2t[...])

    def delta(i, dz, hs):
        s = order3[i]
        done = 0 if i == 0 else order3[i - 1] + b3
        for r, g in groups(b3, 8):
            own = [b for b in range(s + r, s + r + g) if 1 <= b <= L and b >= done]
            for t in range(2):
                cols = slice(t * H, (t + 1) * H)
                d = dz[r * Q:(r + g) * Q, cols].astype(BF16)
                for j in range(4):
                    where = slice(s + r + HZ - 1, s + r + g + HZ - 1)
                    u = u_s[j, where, t].reshape(g * Q, H)
                    sl = s_s[j, where, t].reshape(g * Q, H)
                    hs[t, pl.ds(r * px + j, g * Q, stride=4), :] = (
                        d * pwb[j:j + 1, cols] * sl).astype(F32)
                    if own:
                        a, b = (own[0] - s - r) * Q, (own[-1] + 1 - s - r) * Q
                        m = (d[a:b] * u[a:b]).reshape(len(own), Q, H)
                        part = m[0]
                        for k in range(1, len(own)):
                            part = part + m[k]
                        gpa[j, :, cols] += part.astype(F32)
            for t in range(2):
                dh1e[s + r:s + r + g, t] = (
                    hs[t, r * px:(r + g) * px].astype(BF16).reshape(g, px, H))

    share = L // 4
    bt = max(b for b in range(1, 17) if share % b == 0 and b * px % 128 == 0)

    def turn(upto):
        while turned[0] < L // bt and (turned[0] + 1) * bt + 1 <= upto:
            i = turned[0]
            for t in range(2):
                part = dh1e[1 + i * bt:1 + (i + 1) * bt, t].reshape(bt * px, H)
                dt[t * H:(t + 1) * H, i * bt * px:(i + 1) * bt * px] = part.T
            turned[0] += 1

    turned = [0]

    def first_gradient(c):
        x = stacked(xe, [HX + c * share + k * D1 for k in (-1, 0, 1)], share)
        g = dot(dt[:, c * share * px:(c + 1) * share * px], x)
        if c == 0:
            acc1[...] = g
        elif c < 3:
            acc1[...] += g
        else:
            first_sum[0]([acc1[:, k * C:(k + 1) * C] + g[:, k * C:(k + 1) * C] for k in range(3)])

    def input_gradient_of(b, n):
        parts = [dh1e[pl.ds(at, n), t].reshape(n * px, H)
                 for at in (b + 1 + D1, b + 1, b + 1 - D1) for t in range(2)]
        g = dot(jnp.concatenate(parts, axis=-1), w1t[...])
        dx_ref[pl.ds(b, n)] = g.astype(BF16).reshape(n, px, C)

    first.wait()
    steps = len(order1)
    hs = [hs_a, hs_b]
    h2 = [h2_a, h2_b]
    for i in range(steps):
        if i == inner1:
            for c in halos():
                c.wait()
        if i == min(2, steps - 1):
            for c in second:
                c.wait()
        mix(i, hs[i % 2])
        if i == 0:
            pl.semaphore_wait(barrier, len(targets))
            for c in halos():
                c.start()
        if i == min(2, steps - 1):
            turn_weights(w1, w2, w1t, w2t)
        if i:
            activate(i - 1, hs[(i - 1) % 2])

    reach = order2[0] + b2 + 2 * D2
    apart = order1[-1] + b1 <= order2[0] or reach <= order1[-1]
    early = apart and order2[0] >= HZ and reach <= HZ + L
    if early:
        mix2(0, h2[0])
    activate(steps - 1, hs[(steps - 1) % 2])
    z1e[pl.ds(jnp.where(core == 0, 0, HZ + L), HZ)] = jnp.zeros((HZ, Q, C), BF16)
    if not early:
        mix2(0, h2[0])
    for i in range(len(order2)):
        if i + 1 < len(order2):
            mix2(i + 1, h2[(i + 1) % 2])
        activate2(i, h2[i % 2])

    dz = [dz_a, dz_b]
    mix3(0, dz[0])
    d2 = dh2e[pl.ds(HC, L)].reshape(L * Q, C)
    acc2 = dot_rows(d2, stacked(z1e, [HZ - D2, HZ, HZ + D2], L))
    delta(0, dz[0], hs[0])
    second_sum[0]([acc2[:, k * C:(k + 1) * C] for k in range(3)])
    count = len(order3)
    for i in range(count):
        if i:
            delta(i, dz[i % 2], hs[i % 2])
        if i + 1 < count:
            mix3(i + 1, dz[(i + 1) % 2])
            turn(order3[i] + b3)
            first_gradient(i)
        if i == 1:
            second_sum[1]()

    turn(n3)
    first_gradient(3)
    patch_a()
    dh1e[jnp.where(core == 0, 0, L + 1)] = jnp.zeros((2, px, H), BF16)
    after = [[patch_b], [first_sum[1]], [second_sum[2], patch_c], []]

    def put(q):
        def row(k, value):
            o_ref[q, k] = value
        return row

    for i in range(4):
        input_gradient_of(i * share, share)
        for hook in after[i]:
            hook()
    first_sum[2]()
    patch_d()
    second_sum[3](put(1))
    for c in second_sum[4]() + pairs_p() + plane_p() + line_p() + first_sum[4]():
        c.wait_send()
    first_sum[3](put(0))


def step_pass(scale, ndp, x, cot, w1, w2, pw):
    L, px, C = x.shape
    Q = px // 4
    H = C // 2
    R = C // ndp
    lo_n = divisor(ndp, math.isqrt(ndp))
    hi_n = ndp // lo_n
    n = 2 * (lo_n + 2 * (hi_n - 1) + 1) + lo_n + hi_n - 1
    hbm = pl.BlockSpec(memory_space=pltpu.HBM)
    vm = pl.BlockSpec(memory_space=pltpu.VMEM)
    _, b1, _, _, pieces = first_plan(L)
    b2 = blocks(L + 2 * HC, 3)[0]
    b3 = blocks(L + 2, 4)[0]
    wide = max(b1, b3)

    def sums(lead, w):
        return [
            pltpu.VMEM(lead + (2, lo_n, hi_n, R, w), BF16),
            pltpu.VMEM(lead + (lo_n, hi_n, R, w), BF16),
            pltpu.VMEM(lead + (lo_n - 1, hi_n, R, w), BF16),
            pltpu.VMEM(lead + (lo_n - 1, hi_n, R, w), BF16),
            pltpu.VMEM(lead + (hi_n, R, w), BF16),
            pltpu.VMEM(lead + (2, hi_n, R, w), BF16),
        ]

    limit = 67043328 - (L * px * C * 2 + (1 << 18))
    scratch = [
        pltpu.VMEM((L + 2 * HX, px, C), BF16),
        pltpu.VMEM((L + 2 * HC, Q, C), BF16),
        pltpu.VMEM((L + 2 * HZ, Q, C), BF16),
        pltpu.VMEM((L + 2 * HC, Q, C), BF16),
        pltpu.VMEM((L + 2, 2, px, H), BF16),
        pltpu.VMEM((C, L * px), BF16),
        pltpu.VMEM((4, L + 2 * HZ, 2, Q, H), BF16),
        pltpu.VMEM((4, L + 2 * HZ, 2, Q, H), BF16),
        pltpu.VMEM((2, wide * px, H), F32),
        pltpu.VMEM((2, wide * px, H), F32),
        pltpu.VMEM((b2 * Q, C), F32),
        pltpu.VMEM((b2 * Q, C), F32),
        pltpu.VMEM((b3 * Q, C), F32),
        pltpu.VMEM((b3 * Q, C), F32),
        pltpu.VMEM((3, C, C), BF16),
        pltpu.VMEM((3, C, C), BF16),
        pltpu.VMEM((3 * C, C), BF16),
        pltpu.VMEM((3 * C, C), BF16),
        pltpu.VMEM((4, Q, C), F32),
        pltpu.SemaphoreType.DMA((sum(len(p) for p in pieces),)),
        pltpu.SemaphoreType.DMA((3,)),
        sums((), 3 * H),
        sums((), 3 * H),
        pltpu.VMEM((C, 3 * C), F32),
        pltpu.VMEM((4, C), F32),
        pltpu.VMEM((lo_n, 4, C), F32),
        pltpu.VMEM((hi_n, 4, C), F32),
        pltpu.VMEM((3, 4, C), F32),
        pltpu.SemaphoreType.DMA((2,)),
        pltpu.SemaphoreType.DMA((2,)),
        pltpu.SemaphoreType.DMA((n,)),
        pltpu.SemaphoreType.DMA((n,)),
    ]
    used = sum(math.prod(r.shape) * jnp.dtype(r.dtype).itemsize
               for r in jax.tree.leaves(scratch) if r.memory_space == pltpu.VMEM)
    spare = max((limit - used - (1 << 20)) // (8 * 128 * 4), 1) * 128
    return pl.pallas_call(
        functools.partial(step_kernel, scale, lo_n, hi_n),
        out_shape=(
            pltpu.VMEM((L, px, C), BF16),
            pltpu.VMEM((2, 3, R, C), F32),
            pltpu.VMEM((4, C), F32),
        ),
        in_specs=[hbm] * 4 + [vm],
        out_specs=[vm, vm, vm],
        scratch_shapes=scratch + [pltpu.VMEM((8, spare), F32)],
        compiler_params=pltpu.CompilerParams(
            collective_id=0, has_side_effects=True, vmem_limit_bytes=limit
        ),
        name="step_pass",
    )(x, cot, w1, w2, pw)


def hand_over_kernel(n, dx_ref, o_ref, p_ref, dx_out, o1_out, o2_out, p_out, sem):
    step = dx_ref.shape[0] // n
    out = [pltpu.make_async_copy(dx_ref.at[pl.ds(i * step, step)], dx_out.at[pl.ds(i * step, step)],
                                 sem.at[i]) for i in range(n)]
    for c in out:
        c.start()
    o1_out[...] = o_ref[0]
    o2_out[...] = o_ref[1]
    p_out[...] = p_ref[...]
    for c in out:
        c.wait()


def hand_over(dx, o, p):
    n = divisor(dx.shape[0], 4)
    vm = pl.BlockSpec(memory_space=pltpu.VMEM)
    one = jax.ShapeDtypeStruct(o.shape[1:], F32)
    dx, o1, o2, p = pl.pallas_call(
        functools.partial(hand_over_kernel, n),
        out_shape=(jax.ShapeDtypeStruct(dx.shape, dx.dtype), one, one,
                   jax.ShapeDtypeStruct(p.shape, F32)),
        in_specs=[vm, vm, vm],
        out_specs=[pl.BlockSpec(memory_space=pltpu.HBM), vm, vm, vm],
        scratch_shapes=[pltpu.SemaphoreType.DMA((n,))],
        compiler_params=pltpu.CompilerParams(vmem_limit_bytes=16 * 1024 * 1024),
        name="hand_over",
    )(dx, o, p)
    return dx, jnp.transpose(o1, (1, 0, 2)), jnp.transpose(o2, (1, 0, 2)), p


def shards(ndp, nb, x, w1, w2, pw, cot):
    L, px, C = x.shape
    Q = px // 4
    scale = 1.0 / math.sqrt(L * nb * px * ndp)
    if nb == 2 and ndp >= 4 and (C // ndp) % 16 == 0 and C % 256 == 0 and L >= 48 and L % 8 == 0 and px % 16 == 0:
        return hand_over(*step_pass(scale, ndp, x, cot, w1, w2, pw))
    up = [(i, i + 1) for i in range(nb - 1)]
    down = [(j, i) for i, j in up]

    def edges(x_part, c_part, pairs):
        both = jnp.concatenate([x_part.reshape(HX * px, C), c_part.reshape(HC * Q, C)], axis=0)
        both = lax.ppermute(both, "band", pairs)
        return both[:HX * px].reshape(HX, px, C), both[HX * px:].reshape(HC, Q, C)

    xlo, clo = edges(x[L - HX:], cot[L - HC:], up)
    xhi, chi = edges(x[:HX], cot[:HC], down)
    dx, g, gp = local_pass(nb, x, xlo, xhi, cot, clo, chi, w1, w2, pw)
    kept = lax.psum_scatter(g.astype(F32), "dp", scatter_dimension=1, tiled=True)
    kept = (lax.psum(kept, "band") * scale).reshape(2, C // ndp, 3, C)
    o1, o2 = kept[0], kept[1]
    op = lax.psum(gp, ("dp", "band")) * scale
    return dx, o1, o2, op


def solution(mesh):
    placed = (P("band", "dp", None), P(), P(), P(), P("band", "dp", None))
    return jax.shard_map(
        functools.partial(shards, mesh.shape["dp"], mesh.shape["band"]),
        mesh=mesh,
        in_specs=placed,
        out_specs=(P("band", "dp", None), P("dp", None, None), P("dp", None, None), P()),
        check_vma=False,
    )
```
